256 devices in a mesh: row: 16 (over y_lo, x, core), col: 16 (over y_hi, z).
Axes of the slice: x: 4, y: 4 (y_hi: 2, y_lo: 2; y = y_hi * 2 + y_lo), z: 8, core: 2. Of those that a mesh axis runs over, the one named last changes fastest.
Arguments:
- field: bfloat16 [64, 64, 32, 512], P('row', 'col'), may hold values from -6 to 6
- near_kernel: bfloat16 [9, 2, 2, 256, 256], replicated, may hold values from -0.09375 to 0.09375
- contact: int32 [64, 64, 9], P('row', 'col'), may hold values from 0 to 1
- pillar_shift: int32 [64, 64, 2], P('row', 'col'), may hold values from 0 to 15
- wave_index: int32 [2048, 2], replicated, may hold values from -32 to 31
- wave_form: bfloat16 [2048, 2, 256], replicated, may hold values from -0.25 to 0.25
- wave_weight: float32 [2048], replicated, may hold values from 0.5 to 4
Outputs:
- applied: float32 [64, 64, 32, 512], P('row', 'col')
The draws below stay inside these ranges and needn't reach their ends.
All inputs are finite; a program needn't handle non-finite values.
Results may differ from the reference program's by a relative error of at most 0.0038.
Values may be sent and summed in bfloat16 or wider, within the bound.
A program may use at most 128 MiB of HBM per device.

```python
import math
import jax
import jax.numpy as jnp
from jax import lax

U = 256
W = 2048
S = 32
CLASSES = 2
Q = 16
NRT = 64
NCT = 64


def with_ends(entries, stream_key, smallest, high):
    longest = entries.shape.index(max(entries.shape))
    spots = []
    for shift in (0, 1):
        where = [jax.random.randint(jax.random.fold_in(stream_key, axis), (), 0, length) for axis, length in enumerate(entries.shape)]
        where[longest] = (where[longest] + shift) % entries.shape[longest]
        spots.append(tuple(where))
    return entries.at[spots[0]].set(smallest).at[spots[1]].set(high)


def level_of(stream_key, extent, pieces, least, largest):
    level, own = 1.0, jax.random.fold_in(stream_key, 6)
    for dim, shards_of in pieces:
        heights = jnp.exp(jax.random.uniform(jax.random.fold_in(own, dim), (shards_of,), jnp.float32, least / len(pieces), largest / len(pieces)))
        level = level * jnp.repeat(heights, extent[dim] // shards_of).reshape([-1 if axis == dim else 1 for axis in range(len(extent))])
    return level


def centred(key, shape, width, reach, split=(), held_as=jnp.bfloat16):
    result = width * jax.random.normal(key, shape, jnp.float32)
    if split:
        result = result * level_of(key, shape, split, -0.22, 0.18)
    return jnp.clip(result, -reach, reach).astype(held_as)


def setup_inputs(seed: int = 0) -> dict:
    key_list = jax.random.split(jax.random.key(seed), 8)
    field = centred(key_list[0], (NRT, NCT, S, 2 * U), 1.0, 6.0, ((0, 16), (1, 16)))
    near_kernel = centred(key_list[1], (9, CLASSES, 2, U, U), (18 * U) ** -0.5, 0.09375)
    contact = with_ends(jax.random.randint(key_list[2], (NRT, NCT, 9), 0, CLASSES), jax.random.fold_in(key_list[2], 1), 0, CLASSES - 1).astype(jnp.int32)
    pillar_shift = with_ends(jax.random.randint(key_list[3], (NRT, NCT, 2), 0, Q), jax.random.fold_in(key_list[3], 1), 0, Q - 1).astype(jnp.int32)
    wave_index = with_ends(jax.random.randint(key_list[4], (W, 2), -(NRT // 2), NRT // 2), jax.random.fold_in(key_list[4], 1), -(NRT // 2), (NRT // 2) - 1).astype(jnp.int32)
    wave_form = centred(key_list[5], (W, 2, U), (2 * U) ** -0.5, 0.25)
    wave_weight = jnp.clip(jnp.exp(jax.random.uniform(key_list[6], (W,), jnp.float32, math.log(0.5), math.log(4.0))), 0.5, 4.0)
    return dict(field=field, near_kernel=near_kernel, contact=contact, pillar_shift=pillar_shift, wave_index=wave_index, wave_form=wave_form, wave_weight=wave_weight)


bloch_row = 0.3
bloch_col = 0.17

def realify(real_part, imag_part):
    upper = jnp.concatenate([real_part.T, imag_part.T], axis=1)
    lower = jnp.concatenate([-imag_part.T, real_part.T], axis=1)
    return jnp.concatenate([upper, lower], axis=0)

def wave_angle(wave_index, fine_row, fine_col, row_mod, col_mod):
    order_row = wave_index[:, 0:1]
    order_col = wave_index[:, 1:2]
    turn_row = jnp.mod(order_row * fine_row[None, :], row_mod).astype(jnp.float32) / row_mod
    turn_col = jnp.mod(order_col * fine_col[None, :], col_mod).astype(jnp.float32) / col_mod
    drift = bloch_row * fine_row.astype(jnp.float32) / row_mod + bloch_col * fine_col.astype(jnp.float32) / col_mod
    return 2.0 * math.pi * (turn_row + turn_col + drift[None, :])

def reference(field, near_kernel, contact, pillar_shift, wave_index, wave_form, wave_weight):
    row_mod = Q * NRT
    col_mod = Q * NCT
    wave_matrix = realify(wave_form[:, 0], wave_form[:, 1])
    near_mats = [[realify(near_kernel[offset, variant, 0], near_kernel[offset, variant, 1]) for variant in range(CLASSES)] for offset in range(9)]
    column_ids = jnp.arange(NCT, dtype=jnp.int32)

    def stripe_angles(row_index):
        shifts = lax.dynamic_index_in_dim(pillar_shift, row_index, 0, keepdims=False)
        fine_row = Q * row_index + shifts[:, 0]
        fine_col = Q * column_ids + shifts[:, 1]
        angles = wave_angle(wave_index, fine_row.astype(jnp.int32), fine_col.astype(jnp.int32), row_mod, col_mod)
        return (jnp.cos(angles).T, jnp.sin(angles).T)

    def project(carry, row_index):
        stripe = lax.dynamic_index_in_dim(field, row_index, 0, keepdims=False)
        projected = jnp.dot(stripe.reshape(-1, 2 * U), wave_matrix, preferred_element_type=jnp.float32)
        projected = projected.reshape(NCT, S, 2, W)
        cosine, sine = stripe_angles(row_index)
        hi = lax.Precision.HIGHEST
        coeff_real = jnp.einsum('pw,psw->sw', cosine, projected[:, :, 0], precision=hi) - jnp.einsum('pw,psw->sw', sine, projected[:, :, 1], precision=hi)
        coeff_imag = jnp.einsum('pw,psw->sw', cosine, projected[:, :, 1], precision=hi) + jnp.einsum('pw,psw->sw', sine, projected[:, :, 0], precision=hi)
        return (carry + jnp.stack([coeff_real, coeff_imag], axis=1), None)
    coeff, _ = lax.scan(project, jnp.zeros((S, 2, W), jnp.float32), jnp.arange(NRT, dtype=jnp.int32))
    far_scale = math.sqrt(U / (W * NRT * NCT))
    weighted = ((far_scale * wave_weight)[None, None, :] * coeff).astype(jnp.bfloat16)
    weight_real = weighted[:, 0].astype(jnp.float32)[None]
    weight_imag = weighted[:, 1].astype(jnp.float32)[None]

    def apply_row(row_index):
        near = jnp.zeros((NCT, S, 2 * U), jnp.float32)
        classes = lax.dynamic_index_in_dim(contact, row_index, 0, keepdims=False)
        for offset in range(9):
            step_row = offset // 3 - 1
            step_col = offset % 3 - 1
            source_row = jnp.mod(row_index + step_row, NRT)
            stripe = lax.dynamic_index_in_dim(field, source_row, 0, keepdims=False)
            stripe = jnp.roll(stripe, -step_col, axis=0).reshape(-1, 2 * U)
            for variant in range(CLASSES):
                product = jnp.dot(stripe, near_mats[offset][variant], preferred_element_type=jnp.float32).reshape(NCT, S, 2 * U)
                chosen = (classes[:, offset] == variant)[:, None, None]
                near = near + jnp.where(chosen, product, jnp.float32(0.0))
        cosine, sine = stripe_angles(row_index)
        cos_part = cosine[:, None, :]
        sin_part = sine[:, None, :]
        spread_real = cos_part * weight_real + sin_part * weight_imag
        spread_imag = cos_part * weight_imag - sin_part * weight_real
        spread = jnp.concatenate([spread_real, spread_imag], axis=-1).astype(jnp.bfloat16).reshape(-1, 2 * W)
        far = lax.dot_general(spread, wave_matrix, (((1,), (1,)), ((), ())), preferred_element_type=jnp.float32)
        return near + far.reshape(NCT, S, 2 * U)
    return lax.map(apply_row, jnp.arange(NRT, dtype=jnp.int32))
```

```python
import functools
import math

import jax
import jax.numpy as jnp
from jax import lax
from jax.experimental import pallas as pl
from jax.experimental.pallas import tpu as pltpu
from jax.sharding import PartitionSpec as P

Q = 16
LANES = 128
BLOCH_ROW = 0.3
BLOCH_COL = 0.17
MESH = pl.DeviceIdType.MESH
NT = (((1,), (1,)), ((), ()))

PARTIAL = jnp.float32
NEAR_SPLIT = (0, 3, 5, 7, 9)


def turn_to_cos_sin(turn):
    quarter = jnp.round(turn * 4.0)
    angle = (turn - quarter * 0.25) * (2.0 * math.pi)
    square = angle * angle
    sine = angle * (
        1.0
        + square
        * (-1.0 / 6 + square * (1.0 / 120 + square * (-1.0 / 5040 + square * (1.0 / 362880))))
    )
    cosine = 1.0 + square * (
        -0.5
        + square
        * (1.0 / 24 + square * (-1.0 / 720 + square * (1.0 / 40320 + square * (-1.0 / 3628800))))
    )
    which = quarter.astype(jnp.int32) & 3
    odd = (which & 1) == 1
    c = jnp.where(odd, sine, cosine)
    s = jnp.where(odd, cosine, sine)
    c = jnp.where((which == 1) | (which == 2), -c, c)
    s = jnp.where(which >= 2, -s, s)
    return c, s


def kernel(
    dims,
    field,
    near_kernel,
    contact,
    shift,
    wave_index,
    wave_form,
    wave_weight,
    out,
    xpad,
    form,
    by_wave,
    by_chunk,
    near_mats,
    x2,
    lhs,
    acc,
    cos_all,
    sin_all,
    send1,
    recv1,
    total1,
    send2,
    recv2,
    total2,
    waves_in,
    waves_now,
    local_sem,
    halo_send,
    halo_recv,
    s1,
    r1,
    s2,
    r2,
    s3,
    r3,
    s4,
    r4,
):
    n_row, n_col, rows, cols, sources, waves, unknowns = dims
    pillars = rows * cols
    own = 2 * sources // n_col
    pairs = n_row // 2
    me_row, me_col = lax.axis_index("row"), lax.axis_index("col")
    row_mod, col_mod = Q * rows * n_row, Q * cols * n_col

    def at(row_step, col_step):
        return (lax.rem(me_row + row_step + n_row, n_row), lax.rem(me_col + col_step + n_col, n_col))

    loads = [
        pltpu.make_async_copy(field, xpad.at[1 : rows + 1, 1 : cols + 1], local_sem.at[0]),
        pltpu.make_async_copy(wave_form, form, local_sem.at[1]),
    ]
    for variant in range(2):
        for part in range(2):
            which = 2 * variant + part
            loads.append(
                pltpu.make_async_copy(
                    near_kernel.at[:, variant, part],
                    near_mats.at[:, :, which * unknowns : (which + 1) * unknowns],
                    local_sem.at[2 + which],
                )
            )
    for load in loads:
        load.start()

    barrier = pltpu.get_barrier_semaphore()

    def greet_row(step, _):
        pl.semaphore_signal(
            barrier, inc=1, device_id=(lax.rem(me_row + step, n_row), me_col), device_id_type=MESH
        )
        return 0

    def greet_col(step, _):
        pl.semaphore_signal(
            barrier, inc=1, device_id=(me_row, lax.rem(me_col + step, n_col)), device_id_type=MESH
        )
        return 0

    lax.fori_loop(1, n_row, greet_row, 0)
    lax.fori_loop(1, n_col, greet_col, 0)
    for row_step in (-1, 1):
        for col_step in (-1, 1):
            pl.semaphore_signal(
                barrier, inc=1, device_id=at(row_step, col_step), device_id_type=MESH
            )

    down = lax.broadcasted_iota(jnp.int32, (pillars, LANES), 0)
    fine_row = jnp.zeros((pillars, LANES), jnp.int32)
    fine_col = jnp.zeros((pillars, LANES), jnp.int32)
    for p in range(pillars):
        r, c = divmod(p, cols)
        fine_row = jnp.where(down == p, Q * (me_row * rows + r) + shift[r, 0, c], fine_row)
        fine_col = jnp.where(down == p, Q * (me_col * cols + c) + shift[r, 1, c], fine_col)
    drift = (BLOCH_ROW / row_mod) * fine_row.astype(jnp.float32) + (
        BLOCH_COL / col_mod
    ) * fine_col.astype(jnp.float32)

    def phases(j, _):
        here = pl.ds(pl.multiple_of(j * LANES, LANES), LANES)
        m = wave_index[0:1, here]
        n = wave_index[1:2, here]
        turn_row = ((m * fine_row) & (row_mod - 1)).astype(jnp.float32) * (1.0 / row_mod)
        turn_col = ((n * fine_col) & (col_mod - 1)).astype(jnp.float32) * (1.0 / col_mod)
        c, s = turn_to_cos_sin(turn_row + turn_col + drift)
        cos_all[:, here] = c
        sin_all[:, here] = s
        return 0

    lax.fori_loop(0, waves // LANES, phases, 0)

    to = lax.broadcasted_iota(jnp.int32, (2 * LANES, 2 * LANES), 0)
    source = lax.broadcasted_iota(jnp.int32, (2 * LANES, 2 * LANES), 1)
    wanted = jnp.where(to < LANES, 2 * to, 2 * (to - LANES) + 1)
    apart = jnp.where(source == wanted, 1.0, 0.0).astype(jnp.bfloat16)
    loads[1].wait()

    def split(chunk, _):
        for half in range(2):
            first = pl.multiple_of((2 * chunk + half) * LANES, LANES)
            block = form[pl.ds(first, LANES)].reshape(2 * LANES, unknowns)
            rows_apart = jnp.dot(apart, block, preferred_element_type=jnp.float32)
            rows_apart = rows_apart.astype(jnp.bfloat16)
            by_wave[pl.ds(first, LANES), 0:unknowns] = rows_apart[:LANES]
            by_wave[pl.ds(first, LANES), unknowns : 2 * unknowns] = rows_apart[LANES:]
            by_chunk[chunk, half * LANES : (half + 1) * LANES] = rows_apart[:LANES]
            by_chunk[chunk, (2 + half) * LANES : (3 + half) * LANES] = rows_apart[LANES:]
        return 0

    lax.fori_loop(0, pairs, split, 0)

    loads[0].wait()
    for p in range(pillars):
        r, c = divmod(p, cols)
        x = xpad[1 + r, 1 + c]
        real, imag = x[:, :unknowns], x[:, unknowns:]
        base = 2 * sources * p
        x2[base : base + sources, :unknowns] = real
        x2[base : base + sources, unknowns:] = -imag
        x2[base + sources : base + 2 * sources, :unknowns] = imag
        x2[base + sources : base + 2 * sources, unknowns:] = real

    pl.semaphore_wait(barrier, (n_row - 1) + (n_col - 1) + 4)

    halos = []
    spans = {-1: (slice(0, 1), rows + 1), 1: (slice(rows - 1, rows), 0)}
    col_spans = {-1: (slice(0, 1), cols + 1), 1: (slice(cols - 1, cols), 0)}
    for row_step in (-1, 0, 1):
        for col_step in (-1, 0, 1):
            if (row_step, col_step) == (0, 0):
                continue
            if row_step:
                from_row, into = spans[row_step]
                to_row = slice(into, into + 1)
            else:
                from_row, to_row = slice(0, rows), slice(1, rows + 1)
            if col_step:
                from_col, into = col_spans[col_step]
                to_col = slice(into, into + 1)
            else:
                from_col, to_col = slice(0, cols), slice(1, cols + 1)
            k = len(halos)
            halos.append(
                pltpu.make_async_remote_copy(
                    src_ref=field.at[from_row, from_col],
                    dst_ref=xpad.at[to_row, to_col],
                    send_sem=halo_send.at[k],
                    recv_sem=halo_recv.at[k],
                    device_id=at(row_step, col_step),
                    device_id_type=MESH,
                )
            )
    for halo in halos:
        halo.start()

    def first_copy(peer, slot):
        return pltpu.make_async_remote_copy(
            src_ref=send1.at[peer],
            dst_ref=recv1.at[slot],
            send_sem=s1.at[peer],
            recv_sem=r1.at[slot],
            device_id=(peer, me_col),
            device_id_type=MESH,
        )

    my_pair = lax.div(me_row, 2)

    def project(step, _):
        pair = lax.rem(my_pair + 1 + step, pairs)
        first = pl.multiple_of(pair * 2 * LANES, 2 * LANES)
        projected = lax.dot_general(
            x2[...],
            by_wave[pl.ds(first, 2 * LANES), :],
            NT,
            preferred_element_type=jnp.float32,
        )
        for half in range(2):
            here = pl.ds(pl.multiple_of(first + half * LANES, LANES), LANES)
            lanes = slice(half * LANES, (half + 1) * LANES)
            real = jnp.zeros((sources, LANES), jnp.float32)
            imag = jnp.zeros((sources, LANES), jnp.float32)
            for p in range(pillars):
                base = 2 * sources * p
                pr = projected[base : base + sources, lanes]
                pi = projected[base + sources : base + 2 * sources, lanes]
                c = cos_all[p : p + 1, here]
                s = sin_all[p : p + 1, here]
                real = real + (c * pr - s * pi)
                imag = imag + (c * pi + s * pr)
            peer = 2 * pair + half
            send1[peer, 0:sources] = real.astype(send1.dtype)
            send1[peer, sources : 2 * sources] = imag.astype(send1.dtype)

            @pl.when(peer != me_row)
            def _():
                first_copy(peer, me_row).start()

        return 0

    lax.fori_loop(0, pairs, project, 0)

    def near_offset(offset, _):
        a = lax.div(offset, 3)
        b = lax.rem(offset, 3)
        for p in range(pillars):
            r, c = divmod(p, cols)
            x = xpad[r + a, c + b]
            real, imag = x[:, :unknowns], x[:, unknowns:]
            base = 2 * sources * p
            for variant in range(2):
                mask = jnp.where(contact[r, c, offset] == variant, 1.0, 0.0)
                mask = jnp.full((sources, unknowns), mask, jnp.float32).astype(jnp.bfloat16)
                chosen_real, chosen_imag = real * mask, imag * mask
                low = 2 * variant * unknowns
                mid, high = low + unknowns, low + 2 * unknowns
                lhs[base : base + sources, low:mid] = chosen_real
                lhs[base : base + sources, mid:high] = -chosen_imag
                lhs[base + sources : base + 2 * sources, low:mid] = chosen_imag
                lhs[base + sources : base + 2 * sources, mid:high] = chosen_real
        acc[...] += lax.dot_general(
            lhs[...], near_mats[offset], NT, preferred_element_type=jnp.float32
        )
        return 0

    for load in loads[2:]:
        load.wait()
    for halo in halos:
        halo.wait_recv()
    acc[...] = jnp.zeros_like(acc)
    lax.fori_loop(NEAR_SPLIT[0], NEAR_SPLIT[1], near_offset, 0)

    total1[...] = send1[me_row].astype(jnp.float32)

    def gather1(step, _):
        peer = lax.rem(me_row + step, n_row)
        first_copy(peer, peer).wait_recv()
        total1[...] += recv1[peer].astype(jnp.float32)
        return 0

    lax.fori_loop(1, n_row, gather1, 0)
    for k in range(n_col):
        send2[k] = total1[k * own : (k + 1) * own]

    def second_copy(peer, slot):
        return pltpu.make_async_remote_copy(
            src_ref=send2.at[peer],
            dst_ref=recv2.at[slot],
            send_sem=s2.at[peer],
            recv_sem=r2.at[slot],
            device_id=(me_row, peer),
            device_id_type=MESH,
        )

    def spread2(step, _):
        peer = lax.rem(me_col + step, n_col)
        second_copy(peer, me_col).start()
        return 0

    lax.fori_loop(1, n_col, spread2, 0)
    lax.fori_loop(NEAR_SPLIT[1], NEAR_SPLIT[2], near_offset, 0)

    total2[...] = send2[me_col]

    def gather2(step, _):
        peer = lax.rem(me_col + step, n_col)
        second_copy(peer, peer).wait_recv()
        total2[...] += recv2[peer]
        return 0

    lax.fori_loop(1, n_col, gather2, 0)
    far_scale = math.sqrt(unknowns / (waves * rows * n_row * cols * n_col))
    scale = far_scale * wave_weight[pl.ds(me_row, 1), :]
    waves_in[me_row, me_col] = (scale * total2[...]).astype(jnp.bfloat16)

    def third_copy(peer, slot):
        return pltpu.make_async_remote_copy(
            src_ref=waves_in.at[me_row, me_col],
            dst_ref=waves_in.at[me_row, slot],
            send_sem=s3.at[peer],
            recv_sem=r3.at[slot],
            device_id=(me_row, peer),
            device_id_type=MESH,
        )

    def spread3(step, _):
        peer = lax.rem(me_col + step, n_col)
        third_copy(peer, me_col).start()
        return 0

    lax.fori_loop(1, n_col, spread3, 0)
    lax.fori_loop(NEAR_SPLIT[2], NEAR_SPLIT[3], near_offset, 0)

    def gather3(step, _):
        peer = lax.rem(me_col + step, n_col)
        third_copy(peer, peer).wait_recv()
        return 0

    lax.fori_loop(1, n_col, gather3, 0)

    def fourth_copy(peer, slot):
        return pltpu.make_async_remote_copy(
            src_ref=waves_in.at[me_row],
            dst_ref=waves_in.at[slot],
            send_sem=s4.at[peer],
            recv_sem=r4.at[slot],
            device_id=(peer, me_col),
            device_id_type=MESH,
        )

    def spread4(step, _):
        peer = lax.rem(me_row + step, n_row)
        fourth_copy(peer, me_row).start()
        return 0

    lax.fori_loop(1, n_row, spread4, 0)
    lax.fori_loop(NEAR_SPLIT[3], NEAR_SPLIT[4], near_offset, 0)

    def far_pair(step, _):
        pair = lax.rem(my_pair + step, pairs)
        for half in range(2):
            peer = 2 * pair + half

            @pl.when(peer != me_row)
            def _():
                fourth_copy(peer, peer).wait_recv()

            for k in range(n_col):
                waves_now[half, k * own : (k + 1) * own] = waves_in[peer, k].astype(jnp.float32)
            here = pl.ds(pl.multiple_of((2 * pair + half) * LANES, LANES), LANES)
            wr = waves_now[half, 0:sources]
            wi = waves_now[half, sources : 2 * sources]
            low = slice(half * LANES, (half + 1) * LANES)
            high = slice((2 + half) * LANES, (3 + half) * LANES)
            for p in range(pillars):
                base = 2 * sources * p
                c = cos_all[p : p + 1, here]
                s = sin_all[p : p + 1, here]
                sr = (c * wr + s * wi).astype(jnp.bfloat16)
                si = (c * wi - s * wr).astype(jnp.bfloat16)
                x2[base : base + sources, low] = sr
                x2[base : base + sources, high] = si
                x2[base + sources : base + 2 * sources, low] = si
                x2[base + sources : base + 2 * sources, high] = -sr
        acc[...] += jnp.dot(x2[...], by_chunk[pair], preferred_element_type=jnp.float32)
        return 0

    lax.fori_loop(0, pairs, far_pair, 0)
    for p in range(pillars):
        r, c = divmod(p, cols)
        base = 2 * sources * p
        out[r, c, :, :unknowns] = acc[base : base + sources]
        out[r, c, :, unknowns:] = acc[base + sources : base + 2 * sources]

    for halo in halos:
        halo.wait_send()

    def drain_row(step, _):
        peer = lax.rem(me_row + step, n_row)
        first_copy(peer, me_row).wait_send()
        fourth_copy(peer, me_row).wait_send()
        return 0

    def drain_col(step, _):
        peer = lax.rem(me_col + step, n_col)
        second_copy(peer, me_col).wait_send()
        third_copy(peer, me_col).wait_send()
        return 0

    lax.fori_loop(1, n_row, drain_row, 0)
    lax.fori_loop(1, n_col, drain_col, 0)


def local(field, near_kernel, contact, pillar_shift, wave_index, wave_form, wave_weight):
    rows, cols, sources, width = field.shape
    waves = wave_form.shape[0]
    unknowns = width // 2
    n_row = lax.axis_size("row")
    n_col = lax.axis_size("col")
    own = 2 * sources // n_col
    pillars = rows * cols
    stacked = 2 * pillars * sources
    pairs = n_row // 2
    assert waves == n_row * LANES
    dims = (n_row, n_col, rows, cols, sources, waves, unknowns)
    vmem = pl.BlockSpec(memory_space=pltpu.VMEM)
    smem = pl.BlockSpec(memory_space=pltpu.SMEM)
    anywhere = pl.BlockSpec(memory_space=pl.ANY)
    dma = pltpu.SemaphoreType.DMA
    bf16, f32 = jnp.bfloat16, jnp.float32
    return pl.pallas_call(
        functools.partial(kernel, dims),
        out_shape=jax.ShapeDtypeStruct((rows, cols, sources, width), f32),
        in_specs=[anywhere, anywhere, smem, smem, vmem, anywhere, vmem],
        out_specs=vmem,
        scratch_shapes=[
            pltpu.VMEM((rows + 2, cols + 2, sources, width), bf16),
            pltpu.VMEM((waves, 2, unknowns), bf16),
            pltpu.VMEM((waves, width), bf16),
            pltpu.VMEM((pairs, 4 * LANES, unknowns), bf16),
            pltpu.VMEM((9, unknowns, 4 * unknowns), bf16),
            pltpu.VMEM((stacked, width), bf16),
            pltpu.VMEM((stacked, 2 * width), bf16),
            pltpu.VMEM((stacked, unknowns), f32),
            pltpu.VMEM((pillars, waves), f32),
            pltpu.VMEM((pillars, waves), f32),
            pltpu.VMEM((n_row, 2 * sources, LANES), PARTIAL),
            pltpu.VMEM((n_row, 2 * sources, LANES), PARTIAL),
            pltpu.VMEM((2 * sources, LANES), f32),
            pltpu.VMEM((n_col, own, LANES), f32),
            pltpu.VMEM((n_col, own, LANES), f32),
            pltpu.VMEM((own, LANES), f32),
            pltpu.VMEM((n_row, n_col, own, LANES), bf16),
            pltpu.VMEM((2, 2 * sources, LANES), f32),
            dma((6,)),
            dma((8,)),
            dma((8,)),
            dma((n_row,)),
            dma((n_row,)),
            dma((n_col,)),
            dma((n_col,)),
            dma((n_col,)),
            dma((n_col,)),
            dma((n_row,)),
            dma((n_row,)),
        ],
        compiler_params=pltpu.CompilerParams(
            collective_id=0, has_side_effects=True, vmem_limit_bytes=56 * 1024 * 1024
        ),
        name="bloch_apply",
    )(
        field,
        near_kernel,
        contact,
        pillar_shift.transpose(0, 2, 1),
        wave_index.T,
        wave_form,
        wave_weight.reshape(waves // LANES, LANES),
    )


def solution(mesh):
    placed = (
        P("row", "col", None, None),
        P(),
        P("row", "col", None),
        P("row", "col", None),
        P(),
        P(),
        P(),
    )
    return jax.shard_map(
        local, mesh=mesh, in_specs=placed, out_specs=P("row", "col", None, None), check_vma=False
    )
```

```python
import functools
import math

import jax
import jax.numpy as jnp
from jax import lax
from jax.experimental import pallas as pl
from jax.experimental.pallas import tpu as pltpu
from jax.sharding import PartitionSpec as P

Q = 16
LANES = 128
BLOCH_ROW = 0.3
BLOCH_COL = 0.17
MESH = pl.DeviceIdType.MESH
NT = (((1,), (1,)), ((), ()))

PARTIAL = jnp.float32
NEAR_SPLIT = (0, 1, 5, 9)


def turn_to_cos_sin(turn):
    quarter = jnp.round(turn * 4.0)
    angle = (turn - quarter * 0.25) * (2.0 * math.pi)
    square = angle * angle
    sine = angle * (
        1.0
        + square
        * (-1.0 / 6 + square * (1.0 / 120 + square * (-1.0 / 5040 + square * (1.0 / 362880))))
    )
    cosine = 1.0 + square * (
        -0.5
        + square
        * (1.0 / 24 + square * (-1.0 / 720 + square * (1.0 / 40320 + square * (-1.0 / 3628800))))
    )
    which = quarter.astype(jnp.int32) & 3
    odd = (which & 1) == 1
    c = jnp.where(odd, sine, cosine)
    s = jnp.where(odd, cosine, sine)
    c = jnp.where((which == 1) | (which == 2), -c, c)
    s = jnp.where(which >= 2, -s, s)
    return c, s


def kernel(
    dims,
    field,
    near_kernel,
    contact,
    shift,
    wave_index,
    wave_form,
    wave_weight,
    out,
    xpad,
    form,
    by_wave,
    by_chunk,
    near_mats,
    x2,
    lhs,
    acc,
    cos_all,
    sin_all,
    send1,
    recv1,
    recv2,
    waves_in,
    local_sem,
    halo_send,
    halo_recv,
    s1,
    r1,
    s2,
    r2,
    s3,
    r3,
):
    n_row, n_col, rows, cols, sources, waves, unknowns = dims
    pillars = rows * cols
    quarter = 2 * sources // 4
    pairs = n_row // 2
    me_row, me_col = lax.axis_index("row"), lax.axis_index("col")
    half_cols = n_col // 2
    inner = [(0, 0), (1, 1), (half_cols, 2), (half_cols + 1, 3)]
    outer = list(range(2, half_cols, 2))
    me_q = 2 * lax.div(me_col, half_cols) + lax.rem(me_col, 2)
    me_slot = 4 * me_row + me_q
    peers = 4 * n_row - 1
    row_mod, col_mod = Q * rows * n_row, Q * cols * n_col

    def at(row_step, col_step):
        return (lax.rem(me_row + row_step + n_row, n_row), lax.rem(me_col + col_step + n_col, n_col))

    loads = [
        pltpu.make_async_copy(field, xpad.at[1 : rows + 1, 1 : cols + 1], local_sem.at[0]),
        pltpu.make_async_copy(wave_form, form, local_sem.at[1]),
    ]
    for variant in range(2):
        for part in range(2):
            which = 2 * variant + part
            loads.append(
                pltpu.make_async_copy(
                    near_kernel.at[:, variant, part],
                    near_mats.at[:, :, which * unknowns : (which + 1) * unknowns],
                    local_sem.at[2 + which],
                )
            )
    for load in loads:
        load.start()

    barrier = pltpu.get_barrier_semaphore()

    def greet(row, col):
        pl.semaphore_signal(barrier, inc=1, device_id=(row, col), device_id_type=MESH)

    def greet_row(step, _):
        row = lax.rem(me_row + step, n_row)
        for flip, _q in inner:
            greet(row, jnp.bitwise_xor(me_col, flip))
        return 0

    for flip, _q in inner[1:]:
        greet(me_row, jnp.bitwise_xor(me_col, flip))
    lax.fori_loop(1, n_row, greet_row, 0)
    for flip in outer:
        greet(me_row, jnp.bitwise_xor(me_col, flip))
    steps = [(a, b) for a in (-1, 0, 1) for b in (-1, 0, 1) if (a, b) != (0, 0)]
    for row_step, col_step in steps:
        greet(*at(row_step, col_step))

    down = lax.broadcasted_iota(jnp.int32, (pillars, LANES), 0)
    fine_row = jnp.zeros((pillars, LANES), jnp.int32)
    fine_col = jnp.zeros((pillars, LANES), jnp.int32)
    for p in range(pillars):
        r, c = divmod(p, cols)
        fine_row = jnp.where(down == p, Q * (me_row * rows + r) + shift[r, 0, c], fine_row)
        fine_col = jnp.where(down == p, Q * (me_col * cols + c) + shift[r, 1, c], fine_col)
    drift = (BLOCH_ROW / row_mod) * fine_row.astype(jnp.float32) + (
        BLOCH_COL / col_mod
    ) * fine_col.astype(jnp.float32)

    def phases(j, _):
        here = pl.ds(pl.multiple_of(j * LANES, LANES), LANES)
        m = wave_index[0:1, here]
        n = wave_index[1:2, here]
        turn_row = ((m * fine_row) & (row_mod - 1)).astype(jnp.float32) * (1.0 / row_mod)
        turn_col = ((n * fine_col) & (col_mod - 1)).astype(jnp.float32) * (1.0 / col_mod)
        c, s = turn_to_cos_sin(turn_row + turn_col + drift)
        cos_all[:, here] = c
        sin_all[:, here] = s
        return 0

    lax.fori_loop(0, waves // LANES, phases, 0)

    to = lax.broadcasted_iota(jnp.int32, (2 * LANES, 2 * LANES), 0)
    source = lax.broadcasted_iota(jnp.int32, (2 * LANES, 2 * LANES), 1)
    wanted = jnp.where(to < LANES, 2 * to, 2 * (to - LANES) + 1)
    apart = jnp.where(source == wanted, 1.0, 0.0).astype(jnp.bfloat16)
    loads[1].wait()

    def split(chunk, _):
        for half in range(2):
            first = pl.multiple_of((2 * chunk + half) * LANES, LANES)
            block = form[pl.ds(first, LANES)].reshape(2 * LANES, unknowns)
            rows_apart = jnp.dot(apart, block, preferred_element_type=jnp.float32)
            rows_apart = rows_apart.astype(jnp.bfloat16)
            by_wave[pl.ds(first, LANES), 0:unknowns] = rows_apart[:LANES]
            by_wave[pl.ds(first, LANES), unknowns : 2 * unknowns] = rows_apart[LANES:]
            by_chunk[chunk, half * LANES : (half + 1) * LANES] = rows_apart[:LANES]
            by_chunk[chunk, (2 + half) * LANES : (3 + half) * LANES] = rows_apart[LANES:]
        return 0

    lax.fori_loop(0, pairs, split, 0)

    loads[0].wait()
    for p in range(pillars):
        r, c = divmod(p, cols)
        x = xpad[1 + r, 1 + c]
        real, imag = x[:, :unknowns], x[:, unknowns:]
        base = 2 * sources * p
        x2[base : base + sources, :unknowns] = real
        x2[base : base + sources, unknowns:] = -imag
        x2[base + sources : base + 2 * sources, :unknowns] = imag
        x2[base + sources : base + 2 * sources, unknowns:] = real

    pl.semaphore_wait(barrier, peers + len(outer) + len(steps))

    halos = []
    spans = {-1: (slice(0, 1), rows + 1), 1: (slice(rows - 1, rows), 0)}
    col_spans = {-1: (slice(0, 1), cols + 1), 1: (slice(cols - 1, cols), 0)}
    for row_step, col_step in steps:
        if row_step:
            from_row, into = spans[row_step]
            to_row = slice(into, into + 1)
        else:
            from_row, to_row = slice(0, rows), slice(1, rows + 1)
        if col_step:
            from_col, into = col_spans[col_step]
            to_col = slice(into, into + 1)
        else:
            from_col, to_col = slice(0, cols), slice(1, cols + 1)
        k = len(halos)
        halos.append(
            pltpu.make_async_remote_copy(
                src_ref=field.at[from_row, from_col],
                dst_ref=xpad.at[to_row, to_col],
                send_sem=halo_send.at[k],
                recv_sem=halo_recv.at[k],
                device_id=at(row_step, col_step),
                device_id_type=MESH,
            )
        )

    def first_copy(row, flip, q):
        return pltpu.make_async_remote_copy(
            src_ref=send1.at[4 * row + q],
            dst_ref=recv1.at[me_slot],
            send_sem=s1,
            recv_sem=r1,
            device_id=(row, jnp.bitwise_xor(me_col, flip)),
            device_id_type=MESH,
        )

    def all_first():
        return pltpu.make_async_remote_copy(
            src_ref=send1.at[0:peers],
            dst_ref=recv1.at[0:peers],
            send_sem=s1,
            recv_sem=r1,
            device_id=(me_row, jnp.bitwise_xor(me_col, 1)),
            device_id_type=MESH,
        )

    my_pair = lax.div(me_row, 2)

    def project(step, _):
        pair = lax.rem(my_pair + 1 + step, pairs)
        first = pl.multiple_of(pair * 2 * LANES, 2 * LANES)
        projected = lax.dot_general(
            x2[...],
            by_wave[pl.ds(first, 2 * LANES), :],
            NT,
            preferred_element_type=jnp.float32,
        )
        for half in range(2):
            here = pl.ds(pl.multiple_of(first + half * LANES, LANES), LANES)
            lanes = slice(half * LANES, (half + 1) * LANES)
            real = jnp.zeros((sources, LANES), jnp.float32)
            imag = jnp.zeros((sources, LANES), jnp.float32)
            for p in range(pillars):
                base = 2 * sources * p
                pr = projected[base : base + sources, lanes]
                pi = projected[base + sources : base + 2 * sources, lanes]
                c = cos_all[p : p + 1, here]
                s = sin_all[p : p + 1, here]
                real = real + (c * pr - s * pi)
                imag = imag + (c * pi + s * pr)
            row = 2 * pair + half
            for q in range(4):
                part = (real, imag)[q // 2]
                low = (q % 2) * quarter
                send1[4 * row + q] = part[low : low + quarter].astype(send1.dtype)
            for flip, step_q in inner:
                if flip:
                    first_copy(row, flip, jnp.bitwise_xor(me_q, step_q)).start()
                else:

                    @pl.when(row != me_row)
                    def _():
                        first_copy(row, flip, me_q).start()

        return 0

    lax.fori_loop(0, pairs, project, 0)
    recv1[me_slot] = send1[me_slot]
    for halo in halos:
        halo.start()

    def near_offset(turn, _):
        offset = lax.rem(turn + 4, 9)
        a = lax.div(offset, 3)
        b = lax.rem(offset, 3)
        for p in range(pillars):
            r, c = divmod(p, cols)
            x = xpad[r + a, c + b]
            real, imag = x[:, :unknowns], x[:, unknowns:]
            base = 2 * sources * p
            for variant in range(2):
                mask = jnp.where(contact[r, c, offset] == variant, 1.0, 0.0)
                mask = jnp.full((sources, unknowns), mask, jnp.float32).astype(jnp.bfloat16)
                chosen_real, chosen_imag = real * mask, imag * mask
                low = 2 * variant * unknowns
                mid, high = low + unknowns, low + 2 * unknowns
                lhs[base : base + sources, low:mid] = chosen_real
                lhs[base : base + sources, mid:high] = -chosen_imag
                lhs[base + sources : base + 2 * sources, low:mid] = chosen_imag
                lhs[base + sources : base + 2 * sources, mid:high] = chosen_real
        acc[...] += lax.dot_general(
            lhs[...], near_mats[offset], NT, preferred_element_type=jnp.float32
        )
        return 0

    for load in loads[2:]:
        load.wait()
    acc[...] = jnp.zeros_like(acc)
    lax.fori_loop(NEAR_SPLIT[0], NEAR_SPLIT[1], near_offset, 0)

    all_first().wait_recv()

    def add_row(row, total):
        for q in range(4):
            total = total + recv1[4 * row + q].astype(jnp.float32)
        return total

    recv2[0] = lax.fori_loop(0, n_row, add_row, jnp.zeros((quarter, LANES), jnp.float32))

    seconds = [
        pltpu.make_async_remote_copy(
            src_ref=recv2.at[0],
            dst_ref=recv2.at[1 + k],
            send_sem=s2.at[k],
            recv_sem=r2.at[k],
            device_id=(me_row, jnp.bitwise_xor(me_col, flip)),
            device_id_type=MESH,
        )
        for k, flip in enumerate(outer)
    ]
    for second in seconds:
        second.start()
    for halo in halos:
        halo.wait_recv()
    lax.fori_loop(NEAR_SPLIT[1], NEAR_SPLIT[2], near_offset, 0)
    total = recv2[0]
    for k, second in enumerate(seconds):
        second.wait_recv()
        total = total + recv2[1 + k]

    far_scale = math.sqrt(unknowns / (waves * rows * n_row * cols * n_col))
    scale = far_scale * wave_weight[pl.ds(me_row, 1), :]
    waves_in[me_slot] = (scale * total).astype(jnp.bfloat16)
    my_pair_sem = r3.at[my_pair]

    def third_copy(row, flip):
        return pltpu.make_async_remote_copy(
            src_ref=waves_in.at[me_slot],
            dst_ref=waves_in.at[me_slot],
            send_sem=s3,
            recv_sem=my_pair_sem,
            device_id=(row, jnp.bitwise_xor(me_col, flip)),
            device_id_type=MESH,
        )

    def some_third(first, count, sem):
        return pltpu.make_async_remote_copy(
            src_ref=waves_in.at[pl.ds(first, count)],
            dst_ref=waves_in.at[pl.ds(first, count)],
            send_sem=s3,
            recv_sem=sem,
            device_id=(me_row, jnp.bitwise_xor(me_col, 1)),
            device_id_type=MESH,
        )

    def hand_row(step, _):
        row = lax.rem(me_row + step, n_row)
        for flip, _q in inner:
            third_copy(row, flip).start()
        return 0

    for flip, _q in inner[1:]:
        third_copy(me_row, flip).start()
    lax.fori_loop(1, n_row, hand_row, 0)
    lax.fori_loop(NEAR_SPLIT[2], NEAR_SPLIT[3], near_offset, 0)

    def far_pair(step, _):
        pair = lax.rem(my_pair + step, pairs)

        @pl.when(step == 0)
        def _():
            some_third(0, 7, my_pair_sem).wait_recv()

        @pl.when(step > 0)
        def _():
            some_third(8 * pair, 8, r3.at[pair]).wait_recv()

        for half in range(2):
            here = pl.ds(pl.multiple_of((2 * pair + half) * LANES, LANES), LANES)
            slot = 4 * (2 * pair + half)
            wr = waves_in[pl.ds(slot, 2)].reshape(sources, LANES).astype(jnp.float32)
            wi = waves_in[pl.ds(slot + 2, 2)].reshape(sources, LANES).astype(jnp.float32)
            low = slice(half * LANES, (half + 1) * LANES)
            high = slice((2 + half) * LANES, (3 + half) * LANES)
            for p in range(pillars):
                base = 2 * sources * p
                c = cos_all[p : p + 1, here]
                s = sin_all[p : p + 1, here]
                sr = (c * wr + s * wi).astype(jnp.bfloat16)
                si = (c * wi - s * wr).astype(jnp.bfloat16)
                x2[base : base + sources, low] = sr
                x2[base : base + sources, high] = si
                x2[base + sources : base + 2 * sources, low] = si
                x2[base + sources : base + 2 * sources, high] = -sr
        acc[...] += jnp.dot(x2[...], by_chunk[pair], preferred_element_type=jnp.float32)
        return 0

    lax.fori_loop(0, pairs, far_pair, 0)
    for p in range(pillars):
        r, c = divmod(p, cols)
        base = 2 * sources * p
        out[r, c, :, :unknowns] = acc[base : base + sources]
        out[r, c, :, unknowns:] = acc[base + sources : base + 2 * sources]

    for halo in halos:
        halo.wait_send()

    all_first().wait_send()
    for second in seconds:
        second.wait_send()
    some_third(0, peers, my_pair_sem).wait_send()


def local(field, near_kernel, contact, pillar_shift, wave_index, wave_form, wave_weight):
    rows, cols, sources, width = field.shape
    waves = wave_form.shape[0]
    unknowns = width // 2
    n_row = lax.axis_size("row")
    n_col = lax.axis_size("col")
    quarter = 2 * sources // 4
    pillars = rows * cols
    stacked = 2 * pillars * sources
    pairs = n_row // 2
    assert waves == n_row * LANES
    dims = (n_row, n_col, rows, cols, sources, waves, unknowns)
    vmem = pl.BlockSpec(memory_space=pltpu.VMEM)
    smem = pl.BlockSpec(memory_space=pltpu.SMEM)
    anywhere = pl.BlockSpec(memory_space=pl.ANY)
    dma = pltpu.SemaphoreType.DMA
    bf16, f32 = jnp.bfloat16, jnp.float32
    return pl.pallas_call(
        functools.partial(kernel, dims),
        out_shape=pltpu.VMEM((rows, cols, sources, width), f32),
        in_specs=[anywhere, anywhere, smem, smem, vmem, anywhere, vmem],
        out_specs=vmem,
        scratch_shapes=[
            pltpu.VMEM((rows + 2, cols + 2, sources, width), bf16),
            pltpu.VMEM((waves, 2, unknowns), bf16),
            pltpu.VMEM((waves, width), bf16),
            pltpu.VMEM((pairs, 4 * LANES, unknowns), bf16),
            pltpu.VMEM((9, unknowns, 4 * unknowns), bf16),
            pltpu.VMEM((stacked, width), bf16),
            pltpu.VMEM((stacked, 2 * width), bf16),
            pltpu.VMEM((stacked, unknowns), f32),
            pltpu.VMEM((pillars, waves), f32),
            pltpu.VMEM((pillars, waves), f32),
            pltpu.VMEM((4 * n_row, quarter, LANES), PARTIAL),
            pltpu.VMEM((4 * n_row, quarter, LANES), PARTIAL),
            pltpu.VMEM((max(n_col // 4, 1), quarter, LANES), f32),
            pltpu.VMEM((4 * n_row, quarter, LANES), bf16),
            dma((6,)),
            dma((8,)),
            dma((8,)),
            dma,
            dma,
            dma((max(n_col // 4 - 1, 1),)),
            dma((max(n_col // 4 - 1, 1),)),
            dma,
            dma((pairs,)),
        ],
        compiler_params=pltpu.CompilerParams(
            collective_id=0, has_side_effects=True, vmem_limit_bytes=56 * 1024 * 1024
        ),
        name="bloch_apply",
    )(
        field,
        near_kernel,
        contact,
        pillar_shift.transpose(0, 2, 1),
        wave_index.T,
        wave_form,
        wave_weight.reshape(waves // LANES, LANES),
    )


def solution(mesh):
    placed = (
        P("row", "col", None, None),
        P(),
        P("row", "col", None),
        P("row", "col", None),
        P(),
        P(),
        P(),
    )
    return jax.shard_map(
        local, mesh=mesh, in_specs=placed, out_specs=P("row", "col", None, None), check_vma=False
    )
```

```python
import functools
import math

import jax
import jax.numpy as jnp
from jax import lax
from jax.experimental import pallas as pl
from jax.experimental.pallas import tpu as pltpu
from jax.sharding import PartitionSpec as P

Q = 16
LANES = 128
BLOCH_ROW = 0.3
BLOCH_COL = 0.17
MESH = pl.DeviceIdType.MESH
NT = (((1,), (1,)), ((), ()))

AHEAD = 4
NEAR_SPLIT = (0, 1, 5, 9)


def turn_to_cos_sin(turn):
    quarter = jnp.round(turn * 4.0)
    angle = (turn - quarter * 0.25) * (2.0 * math.pi)
    square = angle * angle
    sine = angle * (
        1.0
        + square
        * (-1.0 / 6 + square * (1.0 / 120 + square * (-1.0 / 5040 + square * (1.0 / 362880))))
    )
    cosine = 1.0 + square * (
        -0.5
        + square
        * (1.0 / 24 + square * (-1.0 / 720 + square * (1.0 / 40320 + square * (-1.0 / 3628800))))
    )
    which = quarter.astype(jnp.int32) & 3
    odd = (which & 1) == 1
    c = jnp.where(odd, sine, cosine)
    s = jnp.where(odd, cosine, sine)
    c = jnp.where((which == 1) | (which == 2), -c, c)
    s = jnp.where(which >= 2, -s, s)
    return c, s


def kernel(
    dims,
    field,
    near_kernel,
    contact,
    shift,
    wave_index,
    wave_form,
    wave_weight,
    out,
    xpad,
    form,
    by_wave,
    by_chunk,
    near_mats,
    x2,
    lhs,
    acc,
    cos_all,
    sin_all,
    partial,
    sibling,
    send1,
    recv1,
    recv2,
    waves_in,
    local_sem,
    halo_send,
    halo_recv,
    s0,
    r0,
    s1,
    r1,
    s2,
    r2,
    s3,
    r3,
):
    n_row, n_col, rows, cols, sources, waves, unknowns = dims
    pillars = rows * cols
    quarter = 2 * sources // 4
    pairs = n_row // 2
    me_row, me_col = lax.axis_index("row"), lax.axis_index("col")
    half_cols = n_col // 2
    inner = [(0, 0), (1, 1), (half_cols, 2), (half_cols + 1, 3)]
    outer = list(range(2, half_cols, 2))
    me_q = 2 * lax.div(me_col, half_cols) + lax.rem(me_col, 2)
    me_slot = 4 * me_row + me_q
    peers = 4 * n_row - 1
    my_pair, me_core = lax.div(me_row, 2), lax.rem(me_row, 2)
    chip_slot = 4 * my_pair + me_q
    chip_peers = 4 * pairs - 1
    row_mod, col_mod = Q * rows * n_row, Q * cols * n_col

    def at(row_step, col_step):
        return (lax.rem(me_row + row_step + n_row, n_row), lax.rem(me_col + col_step + n_col, n_col))

    loads = [
        pltpu.make_async_copy(field, xpad.at[1 : rows + 1, 1 : cols + 1], local_sem.at[0]),
        pltpu.make_async_copy(wave_form, form, local_sem.at[1]),
    ]
    for variant in range(2):
        for part in range(2):
            which = 2 * variant + part
            loads.append(
                pltpu.make_async_copy(
                    near_kernel.at[:, variant, part],
                    near_mats.at[:, :, which * unknowns : (which + 1) * unknowns],
                    local_sem.at[2 + which],
                )
            )
    for load in loads:
        load.start()

    barrier = pltpu.get_barrier_semaphore()

    def greet(row, col):
        pl.semaphore_signal(barrier, inc=1, device_id=(row, col), device_id_type=MESH)

    def greet_row(step, _):
        row = lax.rem(me_row + step, n_row)
        for flip, _q in inner:
            greet(row, jnp.bitwise_xor(me_col, flip))
        return 0

    steps = [(a, b) for a in (-1, 0, 1) for b in (-1, 0, 1) if (a, b) != (0, 0)]
    sideways = [(a, b) for a, b in steps if b]
    for flip in outer:
        greet(me_row, jnp.bitwise_xor(me_col, flip))
    for row_step, col_step in sideways:
        greet(*at(row_step, col_step))
    lax.fori_loop(1, n_row, greet_row, 0)
    for flip, _q in inner[1:]:
        greet(me_row, jnp.bitwise_xor(me_col, flip))

    down = lax.broadcasted_iota(jnp.int32, (pillars, LANES), 0)
    fine_row = jnp.zeros((pillars, LANES), jnp.int32)
    fine_col = jnp.zeros((pillars, LANES), jnp.int32)
    for p in range(pillars):
        r, c = divmod(p, cols)
        fine_row = jnp.where(down == p, Q * (me_row * rows + r) + shift[r, 0, c], fine_row)
        fine_col = jnp.where(down == p, Q * (me_col * cols + c) + shift[r, 1, c], fine_col)
    drift = (BLOCH_ROW / row_mod) * fine_row.astype(jnp.float32) + (
        BLOCH_COL / col_mod
    ) * fine_col.astype(jnp.float32)

    def phases(j, _):
        here = pl.ds(pl.multiple_of(j * LANES, LANES), LANES)
        m = wave_index[0:1, here]
        n = wave_index[1:2, here]
        turn_row = ((m * fine_row) & (row_mod - 1)).astype(jnp.float32) * (1.0 / row_mod)
        turn_col = ((n * fine_col) & (col_mod - 1)).astype(jnp.float32) * (1.0 / col_mod)
        c, s = turn_to_cos_sin(turn_row + turn_col + drift)
        cos_all[:, here] = c
        sin_all[:, here] = s
        return 0

    lax.fori_loop(0, waves // LANES, phases, 0)

    to = lax.broadcasted_iota(jnp.int32, (2 * LANES, 2 * LANES), 0)
    source = lax.broadcasted_iota(jnp.int32, (2 * LANES, 2 * LANES), 1)
    wanted = jnp.where(to < LANES, 2 * to, 2 * (to - LANES) + 1)
    apart = jnp.where(source == wanted, 1.0, 0.0).astype(jnp.bfloat16)
    loads[1].wait()

    def split(chunk, _):
        for half in range(2):
            first = pl.multiple_of((2 * chunk + half) * LANES, LANES)
            block = form[pl.ds(first, LANES)].reshape(2 * LANES, unknowns)
            rows_apart = jnp.dot(apart, block, preferred_element_type=jnp.float32)
            rows_apart = rows_apart.astype(jnp.bfloat16)
            by_wave[pl.ds(first, LANES), 0:unknowns] = rows_apart[:LANES]
            by_wave[pl.ds(first, LANES), unknowns : 2 * unknowns] = rows_apart[LANES:]
            by_chunk[chunk, half * LANES : (half + 1) * LANES] = rows_apart[:LANES]
            by_chunk[chunk, (2 + half) * LANES : (3 + half) * LANES] = rows_apart[LANES:]
        return 0

    lax.fori_loop(0, pairs, split, 0)

    loads[0].wait()
    for p in range(pillars):
        r, c = divmod(p, cols)
        x = xpad[1 + r, 1 + c]
        real, imag = x[:, :unknowns], x[:, unknowns:]
        base = 2 * sources * p
        x2[base : base + sources, :unknowns] = real
        x2[base : base + sources, unknowns:] = -imag
        x2[base + sources : base + 2 * sources, :unknowns] = imag
        x2[base + sources : base + 2 * sources, unknowns:] = real

    halos = []
    spans = {-1: (slice(0, 1), rows + 1), 1: (slice(rows - 1, rows), 0)}
    col_spans = {-1: (slice(0, 1), cols + 1), 1: (slice(cols - 1, cols), 0)}
    for row_step, col_step in steps:
        if row_step:
            from_row, into = spans[row_step]
            to_row = slice(into, into + 1)
        else:
            from_row, to_row = slice(0, rows), slice(1, rows + 1)
        if col_step:
            from_col, into = col_spans[col_step]
            to_col = slice(into, into + 1)
        else:
            from_col, to_col = slice(0, cols), slice(1, cols + 1)
        k = len(halos)
        halos.append(
            pltpu.make_async_remote_copy(
                src_ref=field.at[from_row, from_col],
                dst_ref=xpad.at[to_row, to_col],
                send_sem=halo_send.at[k],
                recv_sem=halo_recv.at[k],
                device_id=at(row_step, col_step),
                device_id_type=MESH,
            )
        )

    def sibling_copy(pair):
        return pltpu.make_async_remote_copy(
            src_ref=partial.at[pair, 1 - me_core],
            dst_ref=sibling.at[pair],
            send_sem=s0.at[pair],
            recv_sem=r0.at[pair],
            device_id=(me_row + 1 - 2 * me_core, me_col),
            device_id_type=MESH,
        )

    def first_copy(pair, flip, q):
        return pltpu.make_async_remote_copy(
            src_ref=send1.at[4 * pair + q],
            dst_ref=recv1.at[chip_slot],
            send_sem=s1,
            recv_sem=r1,
            device_id=(2 * pair + me_core, jnp.bitwise_xor(me_col, flip)),
            device_id_type=MESH,
        )

    def all_first():
        return pltpu.make_async_remote_copy(
            src_ref=send1.at[0:chip_peers],
            dst_ref=recv1.at[0:chip_peers],
            send_sem=s1,
            recv_sem=r1,
            device_id=(me_row, jnp.bitwise_xor(me_col, 1)),
            device_id_type=MESH,
        )

    def pair_at(step):
        return lax.rem(my_pair + 1 + step, pairs)

    def project(step, _):
        pair = pair_at(step)
        first = pl.multiple_of(pair * 2 * LANES, 2 * LANES)
        projected = lax.dot_general(
            x2[...],
            by_wave[pl.ds(first, 2 * LANES), :],
            NT,
            preferred_element_type=jnp.float32,
        )
        for half in range(2):
            here = pl.ds(pl.multiple_of(first + half * LANES, LANES), LANES)
            lanes = slice(half * LANES, (half + 1) * LANES)
            real = jnp.zeros((sources, LANES), jnp.float32)
            imag = jnp.zeros((sources, LANES), jnp.float32)
            for p in range(pillars):
                base = 2 * sources * p
                pr = projected[base : base + sources, lanes]
                pi = projected[base + sources : base + 2 * sources, lanes]
                c = cos_all[p : p + 1, here]
                s = sin_all[p : p + 1, here]
                real = real + (c * pr - s * pi)
                imag = imag + (c * pi + s * pr)
            partial[pair, half, :sources] = real
            partial[pair, half, sources:] = imag
        return 0

    def give(step, _):
        sibling_copy(pair_at(step)).start()
        return 0

    def add_and_send(step, _):
        pair = pair_at(step)
        sibling_copy(pair).wait_recv()
        for q in range(4):
            span = slice(q * quarter, (q + 1) * quarter)
            send1[4 * pair + q] = partial[pair, me_core, span] + sibling[pair, span]
        for flip, step_q in inner:
            if flip:
                first_copy(pair, flip, jnp.bitwise_xor(me_q, step_q)).start()
            else:

                @pl.when(pair != my_pair)
                def _():
                    first_copy(pair, flip, me_q).start()

        return 0

    def project_and_send(step, _):
        project(step, 0)
        give(step, 0)
        add_and_send(step - AHEAD, 0)
        return 0

    ahead = min(AHEAD, pairs)
    lax.fori_loop(0, ahead, project, 0)
    pl.semaphore_wait(barrier, peers + len(outer) + len(sideways))
    lax.fori_loop(0, ahead, give, 0)
    for halo in halos:
        halo.start()
    lax.fori_loop(ahead, pairs, project_and_send, 0)
    lax.fori_loop(pairs - ahead, pairs, add_and_send, 0)
    recv1[chip_slot] = send1[chip_slot]

    def near_offset(turn, _):
        offset = lax.rem(turn + 4, 9)
        a = lax.div(offset, 3)
        b = lax.rem(offset, 3)
        for p in range(pillars):
            r, c = divmod(p, cols)
            x = xpad[r + a, c + b]
            real, imag = x[:, :unknowns], x[:, unknowns:]
            base = 2 * sources * p
            for variant in range(2):
                mask = jnp.where(contact[r, c, offset] == variant, 1.0, 0.0)
                mask = jnp.full((sources, unknowns), mask, jnp.float32).astype(jnp.bfloat16)
                chosen_real, chosen_imag = real * mask, imag * mask
                low = 2 * variant * unknowns
                mid, high = low + unknowns, low + 2 * unknowns
                lhs[base : base + sources, low:mid] = chosen_real
                lhs[base : base + sources, mid:high] = -chosen_imag
                lhs[base + sources : base + 2 * sources, low:mid] = chosen_imag
                lhs[base + sources : base + 2 * sources, mid:high] = chosen_real
        acc[...] += lax.dot_general(
            lhs[...], near_mats[offset], NT, preferred_element_type=jnp.float32
        )
        return 0

    for load in loads[2:]:
        load.wait()
    acc[...] = jnp.zeros_like(acc)
    lax.fori_loop(NEAR_SPLIT[0], NEAR_SPLIT[1], near_offset, 0)

    all_first().wait_recv()

    def add_chip(pair, total):
        for q in range(4):
            total = total + recv1[4 * pair + q]
        return total

    recv2[0] = lax.fori_loop(0, pairs, add_chip, jnp.zeros((quarter, LANES), jnp.float32))

    seconds = [
        pltpu.make_async_remote_copy(
            src_ref=recv2.at[0],
            dst_ref=recv2.at[1 + k],
            send_sem=s2.at[k],
            recv_sem=r2.at[k],
            device_id=(me_row, jnp.bitwise_xor(me_col, flip)),
            device_id_type=MESH,
        )
        for k, flip in enumerate(outer)
    ]
    for second in seconds:
        second.start()
    for halo in halos:
        halo.wait_recv()
    lax.fori_loop(NEAR_SPLIT[1], NEAR_SPLIT[2], near_offset, 0)
    total = recv2[0]
    for k, second in enumerate(seconds):
        second.wait_recv()
        total = total + recv2[1 + k]

    far_scale = math.sqrt(unknowns / (waves * rows * n_row * cols * n_col))
    scale = far_scale * wave_weight[pl.ds(me_row, 1), :]
    waves_in[me_slot] = (scale * total).astype(jnp.bfloat16)
    my_pair_sem = r3.at[my_pair]

    def third_copy(row, flip):
        return pltpu.make_async_remote_copy(
            src_ref=waves_in.at[me_slot],
            dst_ref=waves_in.at[me_slot],
            send_sem=s3,
            recv_sem=my_pair_sem,
            device_id=(row, jnp.bitwise_xor(me_col, flip)),
            device_id_type=MESH,
        )

    def some_third(first, count, sem):
        return pltpu.make_async_remote_copy(
            src_ref=waves_in.at[pl.ds(first, count)],
            dst_ref=waves_in.at[pl.ds(first, count)],
            send_sem=s3,
            recv_sem=sem,
            device_id=(me_row, jnp.bitwise_xor(me_col, 1)),
            device_id_type=MESH,
        )

    def hand_row(step, _):
        row = lax.rem(me_row + step, n_row)
        for flip, _q in inner:
            third_copy(row, flip).start()
        return 0

    for flip, _q in inner[1:]:
        third_copy(me_row, flip).start()
    lax.fori_loop(1, n_row, hand_row, 0)
    lax.fori_loop(NEAR_SPLIT[2], NEAR_SPLIT[3], near_offset, 0)

    def far_pair(step, _):
        pair = lax.rem(my_pair + step, pairs)

        @pl.when(step == 0)
        def _():
            some_third(0, 7, my_pair_sem).wait_recv()

        @pl.when(step > 0)
        def _():
            some_third(8 * pair, 8, r3.at[pair]).wait_recv()

        for half in range(2):
            here = pl.ds(pl.multiple_of((2 * pair + half) * LANES, LANES), LANES)
            slot = 4 * (2 * pair + half)
            wr = waves_in[pl.ds(slot, 2)].reshape(sources, LANES).astype(jnp.float32)
            wi = waves_in[pl.ds(slot + 2, 2)].reshape(sources, LANES).astype(jnp.float32)
            low = slice(half * LANES, (half + 1) * LANES)
            high = slice((2 + half) * LANES, (3 + half) * LANES)
            for p in range(pillars):
                base = 2 * sources * p
                c = cos_all[p : p + 1, here]
                s = sin_all[p : p + 1, here]
                sr = (c * wr + s * wi).astype(jnp.bfloat16)
                si = (c * wi - s * wr).astype(jnp.bfloat16)
                x2[base : base + sources, low] = sr
                x2[base : base + sources, high] = si
                x2[base + sources : base + 2 * sources, low] = si
                x2[base + sources : base + 2 * sources, high] = -sr
        acc[...] += jnp.dot(x2[...], by_chunk[pair], preferred_element_type=jnp.float32)
        return 0

    lax.fori_loop(0, pairs, far_pair, 0)
    for p in range(pillars):
        r, c = divmod(p, cols)
        base = 2 * sources * p
        out[r, c, :, :unknowns] = acc[base : base + sources]
        out[r, c, :, unknowns:] = acc[base + sources : base + 2 * sources]

    for halo in halos:
        halo.wait_send()

    def drain(pair, _):
        sibling_copy(pair).wait_send()
        return 0

    lax.fori_loop(0, pairs, drain, 0)
    all_first().wait_send()
    for second in seconds:
        second.wait_send()
    some_third(0, peers, my_pair_sem).wait_send()


def local(field, near_kernel, contact, pillar_shift, wave_index, wave_form, wave_weight):
    rows, cols, sources, width = field.shape
    waves = wave_form.shape[0]
    unknowns = width // 2
    n_row = lax.axis_size("row")
    n_col = lax.axis_size("col")
    quarter = 2 * sources // 4
    pillars = rows * cols
    stacked = 2 * pillars * sources
    pairs = n_row // 2
    assert waves == n_row * LANES
    dims = (n_row, n_col, rows, cols, sources, waves, unknowns)
    vmem = pl.BlockSpec(memory_space=pltpu.VMEM)
    smem = pl.BlockSpec(memory_space=pltpu.SMEM)
    anywhere = pl.BlockSpec(memory_space=pl.ANY)
    dma = pltpu.SemaphoreType.DMA
    bf16, f32 = jnp.bfloat16, jnp.float32
    return pl.pallas_call(
        functools.partial(kernel, dims),
        out_shape=pltpu.VMEM((rows, cols, sources, width), f32),
        in_specs=[anywhere, anywhere, smem, smem, vmem, anywhere, vmem],
        out_specs=vmem,
        scratch_shapes=[
            pltpu.VMEM((rows + 2, cols + 2, sources, width), bf16),
            pltpu.VMEM((waves, 2, unknowns), bf16),
            pltpu.VMEM((waves, width), bf16),
            pltpu.VMEM((pairs, 4 * LANES, unknowns), bf16),
            pltpu.VMEM((9, unknowns, 4 * unknowns), bf16),
            pltpu.VMEM((stacked, width), bf16),
            pltpu.VMEM((stacked, 2 * width), bf16),
            pltpu.VMEM((stacked, unknowns), f32),
            pltpu.VMEM((pillars, waves), f32),
            pltpu.VMEM((pillars, waves), f32),
            pltpu.VMEM((pairs, 2, 2 * sources, LANES), f32),
            pltpu.VMEM((pairs, 2 * sources, LANES), f32),
            pltpu.VMEM((4 * pairs, quarter, LANES), f32),
            pltpu.VMEM((4 * pairs, quarter, LANES), f32),
            pltpu.VMEM((max(n_col // 4, 1), quarter, LANES), f32),
            pltpu.VMEM((4 * n_row, quarter, LANES), bf16),
            dma((6,)),
            dma((8,)),
            dma((8,)),
            dma((pairs,)),
            dma((pairs,)),
            dma,
            dma,
            dma((max(n_col // 4 - 1, 1),)),
            dma((max(n_col // 4 - 1, 1),)),
            dma,
            dma((pairs,)),
        ],
        compiler_params=pltpu.CompilerParams(
            collective_id=0, has_side_effects=True, vmem_limit_bytes=56 * 1024 * 1024
        ),
        name="bloch_apply",
    )(
        field,
        near_kernel,
        contact,
        pillar_shift.transpose(0, 2, 1),
        wave_index.T,
        wave_form,
        wave_weight.reshape(waves // LANES, LANES),
    )


def solution(mesh):
    placed = (
        P("row", "col", None, None),
        P(),
        P("row", "col", None),
        P("row", "col", None),
        P(),
        P(),
        P(),
    )
    return jax.shard_map(
        local, mesh=mesh, in_specs=placed, out_specs=P("row", "col", None, None), check_vma=False
    )
```

```python
import functools
import math

import jax
import jax.numpy as jnp
from jax import lax
from jax.experimental import pallas as pl
from jax.experimental.pallas import tpu as pltpu
from jax.sharding import PartitionSpec as P

Q = 16
LANES = 128
BLOCH_ROW = 0.3
BLOCH_COL = 0.17
MESH = pl.DeviceIdType.MESH
NT = (((1,), (1,)), ((), ()))

AHEAD = 4


def turn_to_cos_sin(turn):
    quarter = jnp.round(turn * 4.0)
    angle = (turn - quarter * 0.25) * (2.0 * math.pi)
    square = angle * angle
    sine = angle * (
        1.0
        + square
        * (-1.0 / 6 + square * (1.0 / 120 + square * (-1.0 / 5040 + square * (1.0 / 362880))))
    )
    cosine = 1.0 + square * (
        -0.5
        + square
        * (1.0 / 24 + square * (-1.0 / 720 + square * (1.0 / 40320 + square * (-1.0 / 3628800))))
    )
    which = quarter.astype(jnp.int32) & 3
    odd = (which & 1) == 1
    c = jnp.where(odd, sine, cosine)
    s = jnp.where(odd, cosine, sine)
    c = jnp.where((which == 1) | (which == 2), -c, c)
    s = jnp.where(which >= 2, -s, s)
    return c, s


def kernel(
    dims,
    field,
    near_kernel,
    contact,
    shift,
    wave_index,
    wave_form,
    wave_weight,
    out,
    xpad,
    form,
    by_wave,
    by_chunk,
    near_mats,
    x2,
    lhs,
    acc,
    cos_all,
    sin_all,
    partial,
    sibling,
    send1,
    recv1,
    recv2,
    waves_in,
    local_sem,
    halo_send,
    halo_recv,
    s0,
    r0,
    s1,
    r1,
    s2,
    r2,
    s3,
    r3,
):
    n_row, n_col, rows, cols, sources, waves, unknowns = dims
    pillars = rows * cols
    quarter = 2 * sources // 4
    pairs = n_row // 2
    me_row, me_col = lax.axis_index("row"), lax.axis_index("col")
    half_cols = n_col // 2
    inner = [(0, 0), (1, 1), (half_cols, 2), (half_cols + 1, 3)]
    outer = list(range(2, half_cols, 2))
    me_q = 2 * lax.div(me_col, half_cols) + lax.rem(me_col, 2)
    me_slot = 4 * me_row + me_q
    peers = 4 * n_row - 1
    my_pair, me_core = lax.div(me_row, 2), lax.rem(me_row, 2)
    chip_slot = 4 * my_pair + me_q
    chip_peers = 4 * pairs - 1
    row_mod, col_mod = Q * rows * n_row, Q * cols * n_col

    def at(row_step, col_step):
        return (lax.rem(me_row + row_step + n_row, n_row), lax.rem(me_col + col_step + n_col, n_col))

    loads = [
        pltpu.make_async_copy(field, xpad.at[1 : rows + 1, 1 : cols + 1], local_sem.at[0]),
        pltpu.make_async_copy(wave_form, form, local_sem.at[1]),
    ]
    for variant in range(2):
        for part in range(2):
            which = 2 * variant + part
            loads.append(
                pltpu.make_async_copy(
                    near_kernel.at[:, variant, part],
                    near_mats.at[:, :, which * unknowns : (which + 1) * unknowns],
                    local_sem.at[2 + which],
                )
            )
    for load in loads:
        load.start()

    barrier = pltpu.get_barrier_semaphore()

    def greet(row, col):
        pl.semaphore_signal(barrier, inc=1, device_id=(row, col), device_id_type=MESH)

    def greet_row(step, _):
        row = lax.rem(me_row + step, n_row)
        for flip, _q in inner:
            greet(row, jnp.bitwise_xor(me_col, flip))
        return 0

    steps = [(0, -1), (0, 1), (-1, 0), (1, 0)]
    sideways = steps[:2]
    for flip in outer:
        greet(me_row, jnp.bitwise_xor(me_col, flip))
    for row_step, col_step in sideways:
        greet(*at(row_step, col_step))
    lax.fori_loop(1, n_row, greet_row, 0)
    for flip, _q in inner[1:]:
        greet(me_row, jnp.bitwise_xor(me_col, flip))

    down = lax.broadcasted_iota(jnp.int32, (pillars, LANES), 0)
    fine_row = jnp.zeros((pillars, LANES), jnp.int32)
    fine_col = jnp.zeros((pillars, LANES), jnp.int32)
    for p in range(pillars):
        r, c = divmod(p, cols)
        fine_row = jnp.where(down == p, Q * (me_row * rows + r) + shift[r, 0, c], fine_row)
        fine_col = jnp.where(down == p, Q * (me_col * cols + c) + shift[r, 1, c], fine_col)
    drift = (BLOCH_ROW / row_mod) * fine_row.astype(jnp.float32) + (
        BLOCH_COL / col_mod
    ) * fine_col.astype(jnp.float32)

    def phases(j, _):
        here = pl.ds(pl.multiple_of(j * LANES, LANES), LANES)
        m = wave_index[0:1, here]
        n = wave_index[1:2, here]
        turn_row = ((m * fine_row) & (row_mod - 1)).astype(jnp.float32) * (1.0 / row_mod)
        turn_col = ((n * fine_col) & (col_mod - 1)).astype(jnp.float32) * (1.0 / col_mod)
        c, s = turn_to_cos_sin(turn_row + turn_col + drift)
        cos_all[:, here] = c
        sin_all[:, here] = s
        return 0

    lax.fori_loop(0, waves // LANES, phases, 0)

    to = lax.broadcasted_iota(jnp.int32, (2 * LANES, 2 * LANES), 0)
    source = lax.broadcasted_iota(jnp.int32, (2 * LANES, 2 * LANES), 1)
    wanted = jnp.where(to < LANES, 2 * to, 2 * (to - LANES) + 1)
    apart = jnp.where(source == wanted, 1.0, 0.0).astype(jnp.bfloat16)
    loads[1].wait()

    def split(chunk, _):
        for half in range(2):
            first = pl.multiple_of((2 * chunk + half) * LANES, LANES)
            block = form[pl.ds(first, LANES)].reshape(2 * LANES, unknowns)
            rows_apart = jnp.dot(apart, block, preferred_element_type=jnp.float32)
            rows_apart = rows_apart.astype(jnp.bfloat16)
            by_wave[pl.ds(first, LANES), 0:unknowns] = rows_apart[:LANES]
            by_wave[pl.ds(first, LANES), unknowns : 2 * unknowns] = rows_apart[LANES:]
            by_chunk[chunk, half * LANES : (half + 1) * LANES] = rows_apart[:LANES]
            by_chunk[chunk, (2 + half) * LANES : (3 + half) * LANES] = rows_apart[LANES:]
        return 0

    lax.fori_loop(0, pairs, split, 0)

    loads[0].wait()
    for p in range(pillars):
        r, c = divmod(p, cols)
        x = xpad[1 + r, 1 + c]
        real, imag = x[:, :unknowns], x[:, unknowns:]
        base = 2 * sources * p
        x2[base : base + sources, :unknowns] = real
        x2[base : base + sources, unknowns:] = -imag
        x2[base + sources : base + 2 * sources, :unknowns] = imag
        x2[base + sources : base + 2 * sources, unknowns:] = real

    halos = []
    spans = {-1: (slice(0, 1), rows + 1), 1: (slice(rows - 1, rows), 0)}
    col_spans = {-1: (slice(0, 1), cols + 1), 1: (slice(cols - 1, cols), 0)}
    for row_step, col_step in steps:
        if row_step:
            from_row, into = spans[row_step]
            to_row = slice(into, into + 1)
        else:
            from_row, to_row = slice(0, rows), slice(1, rows + 1)
        if col_step:
            from_col, into = col_spans[col_step]
            to_col = slice(into, into + 1)
        else:
            from_col, to_col = slice(0, cols), slice(1, cols + 1)
        k = len(halos)
        halos.append(
            pltpu.make_async_remote_copy(
                src_ref=field.at[from_row, from_col],
                dst_ref=xpad.at[to_row, to_col],
                send_sem=halo_send.at[k],
                recv_sem=halo_recv.at[k],
                device_id=at(row_step, col_step),
                device_id_type=MESH,
            )
        )

    corners = []
    for row_step in (-1, 1):
        from_row, into = spans[row_step]
        for edge in (0, cols + 1):
            k = len(halos) + len(corners)
            corners.append(
                pltpu.make_async_remote_copy(
                    src_ref=xpad.at[1 + from_row.start, edge],
                    dst_ref=xpad.at[into, edge],
                    send_sem=halo_send.at[k],
                    recv_sem=halo_recv.at[k],
                    device_id=at(row_step, 0),
                    device_id_type=MESH,
                )
            )

    def sibling_copy(pair):
        return pltpu.make_async_remote_copy(
            src_ref=partial.at[pair, 1 - me_core],
            dst_ref=sibling.at[pair],
            send_sem=s0.at[pair],
            recv_sem=r0.at[pair],
            device_id=(me_row + 1 - 2 * me_core, me_col),
            device_id_type=MESH,
        )

    def first_copy(pair, flip, q):
        return pltpu.make_async_remote_copy(
            src_ref=send1.at[4 * pair + q],
            dst_ref=recv1.at[chip_slot],
            send_sem=s1,
            recv_sem=r1,
            device_id=(2 * pair + me_core, jnp.bitwise_xor(me_col, flip)),
            device_id_type=MESH,
        )

    def all_first():
        return pltpu.make_async_remote_copy(
            src_ref=send1.at[0:chip_peers],
            dst_ref=recv1.at[0:chip_peers],
            send_sem=s1,
            recv_sem=r1,
            device_id=(me_row, jnp.bitwise_xor(me_col, 1)),
            device_id_type=MESH,
        )

    def pair_at(step):
        return lax.rem(my_pair + 1 + step, pairs)

    def project(step, _):
        pair = pair_at(step)
        first = pl.multiple_of(pair * 2 * LANES, 2 * LANES)
        projected = lax.dot_general(
            x2[...],
            by_wave[pl.ds(first, 2 * LANES), :],
            NT,
            preferred_element_type=jnp.float32,
        )
        for half in range(2):
            here = pl.ds(pl.multiple_of(first + half * LANES, LANES), LANES)
            lanes = slice(half * LANES, (half + 1) * LANES)
            real = jnp.zeros((sources, LANES), jnp.float32)
            imag = jnp.zeros((sources, LANES), jnp.float32)
            for p in range(pillars):
                base = 2 * sources * p
                pr = projected[base : base + sources, lanes]
                pi = projected[base + sources : base + 2 * sources, lanes]
                c = cos_all[p : p + 1, here]
                s = sin_all[p : p + 1, here]
                real = real + (c * pr - s * pi)
                imag = imag + (c * pi + s * pr)
            partial[pair, half, :sources] = real
            partial[pair, half, sources:] = imag
        return 0

    def give(step, _):
        sibling_copy(pair_at(step)).start()
        return 0

    def add_and_send(step, _):
        pair = pair_at(step)
        sibling_copy(pair).wait_recv()
        for q in range(4):
            span = slice(q * quarter, (q + 1) * quarter)
            send1[4 * pair + q] = partial[pair, me_core, span] + sibling[pair, span]
        for flip, step_q in inner:
            if flip:
                first_copy(pair, flip, jnp.bitwise_xor(me_q, step_q)).start()
            else:

                @pl.when(pair != my_pair)
                def _():
                    first_copy(pair, flip, me_q).start()

        return 0

    def project_and_send(step, _):
        project(step, 0)
        give(step, 0)
        add_and_send(step - AHEAD, 0)
        return 0

    ahead = min(AHEAD, pairs)
    lax.fori_loop(0, ahead, project, 0)
    pl.semaphore_wait(barrier, peers + len(outer) + len(sideways))
    lax.fori_loop(0, ahead, give, 0)
    for halo in halos:
        halo.start()
    lax.fori_loop(ahead, pairs, project_and_send, 0)
    lax.fori_loop(pairs - ahead, pairs, add_and_send, 0)
    recv1[chip_slot] = send1[chip_slot]

    def near_offset(offset):
        a = lax.div(offset, 3)
        b = lax.rem(offset, 3)
        for p in range(pillars):
            r, c = divmod(p, cols)
            x = xpad[r + a, c + b]
            real, imag = x[:, :unknowns], x[:, unknowns:]
            base = 2 * sources * p
            for variant in range(2):
                mask = jnp.where(contact[r, c, offset] == variant, 1.0, 0.0)
                mask = jnp.full((sources, unknowns), mask, jnp.float32).astype(jnp.bfloat16)
                chosen_real, chosen_imag = real * mask, imag * mask
                low = 2 * variant * unknowns
                mid, high = low + unknowns, low + 2 * unknowns
                lhs[base : base + sources, low:mid] = chosen_real
                lhs[base : base + sources, mid:high] = -chosen_imag
                lhs[base + sources : base + 2 * sources, low:mid] = chosen_imag
                lhs[base + sources : base + 2 * sources, mid:high] = chosen_real
        acc[...] += lax.dot_general(
            lhs[...], near_mats[offset], NT, preferred_element_type=jnp.float32
        )

    def near_edge(turn, _):
        near_offset(2 * turn + 1)
        return 0

    def near_corner(turn, _):
        near_offset(2 * turn + 2 * lax.div(turn, 2))
        return 0

    for load in loads[2:]:
        load.wait()
    acc[...] = jnp.zeros_like(acc)
    near_offset(jnp.int32(4))

    all_first().wait_recv()

    def add_chip(pair, total):
        for q in range(4):
            total = total + recv1[4 * pair + q]
        return total

    recv2[0] = lax.fori_loop(0, pairs, add_chip, jnp.zeros((quarter, LANES), jnp.float32))

    seconds = [
        pltpu.make_async_remote_copy(
            src_ref=recv2.at[0],
            dst_ref=recv2.at[1 + k],
            send_sem=s2.at[k],
            recv_sem=r2.at[k],
            device_id=(me_row, jnp.bitwise_xor(me_col, flip)),
            device_id_type=MESH,
        )
        for k, flip in enumerate(outer)
    ]
    for second in seconds:
        second.start()
    for halo in halos:
        halo.wait_recv()
    for corner in corners:
        corner.start()
    lax.fori_loop(0, 4, near_edge, 0)
    total = recv2[0]
    for k, second in enumerate(seconds):
        second.wait_recv()
        total = total + recv2[1 + k]

    far_scale = math.sqrt(unknowns / (waves * rows * n_row * cols * n_col))
    scale = far_scale * wave_weight[pl.ds(me_row, 1), :]
    waves_in[me_slot] = (scale * total).astype(jnp.bfloat16)
    my_pair_sem = r3.at[my_pair]

    def third_copy(row, flip):
        return pltpu.make_async_remote_copy(
            src_ref=waves_in.at[me_slot],
            dst_ref=waves_in.at[me_slot],
            send_sem=s3,
            recv_sem=my_pair_sem,
            device_id=(row, jnp.bitwise_xor(me_col, flip)),
            device_id_type=MESH,
        )

    def some_third(first, count, sem):
        return pltpu.make_async_remote_copy(
            src_ref=waves_in.at[pl.ds(first, count)],
            dst_ref=waves_in.at[pl.ds(first, count)],
            send_sem=s3,
            recv_sem=sem,
            device_id=(me_row, jnp.bitwise_xor(me_col, 1)),
            device_id_type=MESH,
        )

    def hand_row(step, _):
        row = lax.rem(me_row + step, n_row)
        for flip, _q in inner:
            third_copy(row, flip).start()
        return 0

    for flip, _q in inner[1:]:
        third_copy(me_row, flip).start()
    lax.fori_loop(1, n_row, hand_row, 0)
    for corner in corners:
        corner.wait_recv()
    lax.fori_loop(0, 4, near_corner, 0)

    def far_pair(step, _):
        pair = lax.rem(my_pair - step + pairs, pairs)

        @pl.when(step == 0)
        def _():
            some_third(0, 7, my_pair_sem).wait_recv()

        @pl.when(step > 0)
        def _():
            some_third(8 * pair, 8, r3.at[pair]).wait_recv()

        for half in range(2):
            here = pl.ds(pl.multiple_of((2 * pair + half) * LANES, LANES), LANES)
            slot = 4 * (2 * pair + half)
            wr = waves_in[pl.ds(slot, 2)].reshape(sources, LANES).astype(jnp.float32)
            wi = waves_in[pl.ds(slot + 2, 2)].reshape(sources, LANES).astype(jnp.float32)
            low = slice(half * LANES, (half + 1) * LANES)
            high = slice((2 + half) * LANES, (3 + half) * LANES)
            for p in range(pillars):
                base = 2 * sources * p
                c = cos_all[p : p + 1, here]
                s = sin_all[p : p + 1, here]
                sr = (c * wr + s * wi).astype(jnp.bfloat16)
                si = (c * wi - s * wr).astype(jnp.bfloat16)
                x2[base : base + sources, low] = sr
                x2[base : base + sources, high] = si
                x2[base + sources : base + 2 * sources, low] = si
                x2[base + sources : base + 2 * sources, high] = -sr
        acc[...] += jnp.dot(x2[...], by_chunk[pair], preferred_element_type=jnp.float32)
        return 0

    lax.fori_loop(0, pairs, far_pair, 0)
    for p in range(pillars):
        r, c = divmod(p, cols)
        base = 2 * sources * p
        out[r, c, :, :unknowns] = acc[base : base + sources]
        out[r, c, :, unknowns:] = acc[base + sources : base + 2 * sources]

    for halo in halos + corners:
        halo.wait_send()

    def drain(pair, _):
        sibling_copy(pair).wait_send()
        return 0

    lax.fori_loop(0, pairs, drain, 0)
    all_first().wait_send()
    for second in seconds:
        second.wait_send()
    some_third(0, peers, my_pair_sem).wait_send()


def local(field, near_kernel, contact, pillar_shift, wave_index, wave_form, wave_weight):
    rows, cols, sources, width = field.shape
    waves = wave_form.shape[0]
    unknowns = width // 2
    n_row = lax.axis_size("row")
    n_col = lax.axis_size("col")
    quarter = 2 * sources // 4
    pillars = rows * cols
    stacked = 2 * pillars * sources
    pairs = n_row // 2
    assert waves == n_row * LANES
    dims = (n_row, n_col, rows, cols, sources, waves, unknowns)
    vmem = pl.BlockSpec(memory_space=pltpu.VMEM)
    smem = pl.BlockSpec(memory_space=pltpu.SMEM)
    anywhere = pl.BlockSpec(memory_space=pl.ANY)
    dma = pltpu.SemaphoreType.DMA
    bf16, f32 = jnp.bfloat16, jnp.float32
    return pl.pallas_call(
        functools.partial(kernel, dims),
        out_shape=pltpu.VMEM((rows, cols, sources, width), f32),
        in_specs=[anywhere, anywhere, smem, smem, vmem, anywhere, vmem],
        out_specs=vmem,
        scratch_shapes=[
            pltpu.VMEM((rows + 2, cols + 2, sources, width), bf16),
            pltpu.VMEM((waves, 2, unknowns), bf16),
            pltpu.VMEM((waves, width), bf16),
            pltpu.VMEM((pairs, 4 * LANES, unknowns), bf16),
            pltpu.VMEM((9, unknowns, 4 * unknowns), bf16),
            pltpu.VMEM((stacked, width), bf16),
            pltpu.VMEM((stacked, 2 * width), bf16),
            pltpu.VMEM((stacked, unknowns), f32),
            pltpu.VMEM((pillars, waves), f32),
            pltpu.VMEM((pillars, waves), f32),
            pltpu.VMEM((pairs, 2, 2 * sources, LANES), f32),
            pltpu.VMEM((pairs, 2 * sources, LANES), f32),
            pltpu.VMEM((4 * pairs, quarter, LANES), f32),
            pltpu.VMEM((4 * pairs, quarter, LANES), f32),
            pltpu.VMEM((max(n_col // 4, 1), quarter, LANES), f32),
            pltpu.VMEM((4 * n_row, quarter, LANES), bf16),
            dma((6,)),
            dma((8,)),
            dma((8,)),
            dma((pairs,)),
            dma((pairs,)),
            dma,
            dma,
            dma((max(n_col // 4 - 1, 1),)),
            dma((max(n_col // 4 - 1, 1),)),
            dma,
            dma((pairs,)),
        ],
        compiler_params=pltpu.CompilerParams(
            collective_id=0, has_side_effects=True, vmem_limit_bytes=56 * 1024 * 1024
        ),
        name="bloch_apply",
    )(
        field,
        near_kernel,
        contact,
        pillar_shift.transpose(0, 2, 1),
        wave_index.T,
        wave_form,
        wave_weight.reshape(waves // LANES, LANES),
    )


def solution(mesh):
    placed = (
        P("row", "col", None, None),
        P(),
        P("row", "col", None),
        P("row", "col", None),
        P(),
        P(),
        P(),
    )
    return jax.shard_map(
        local, mesh=mesh, in_specs=placed, out_specs=P("row", "col", None, None), check_vma=False
    )
```

```python
import functools
import math

import jax
import jax.numpy as jnp
from jax import lax
from jax.experimental import pallas as pl
from jax.experimental.pallas import tpu as pltpu
from jax.sharding import PartitionSpec as P

Q = 16
LANES = 128
BLOCH_ROW = 0.3
BLOCH_COL = 0.17
MESH = pl.DeviceIdType.MESH
NT = (((1,), (1,)), ((), ()))

AHEAD = 2


def turn_to_cos_sin(turn):
    quarter = jnp.round(turn * 4.0)
    angle = (turn - quarter * 0.25) * (2.0 * math.pi)
    square = angle * angle
    sine = angle * (
        1.0
        + square
        * (-1.0 / 6 + square * (1.0 / 120 + square * (-1.0 / 5040 + square * (1.0 / 362880))))
    )
    cosine = 1.0 + square * (
        -0.5
        + square
        * (1.0 / 24 + square * (-1.0 / 720 + square * (1.0 / 40320 + square * (-1.0 / 3628800))))
    )
    which = quarter.astype(jnp.int32) & 3
    odd = (which & 1) == 1
    c = jnp.where(odd, sine, cosine)
    s = jnp.where(odd, cosine, sine)
    c = jnp.where((which == 1) | (which == 2), -c, c)
    s = jnp.where(which >= 2, -s, s)
    return c, s


def kernel(
    dims,
    field,
    near_kernel,
    contact,
    shift,
    wave_index,
    wave_form,
    wave_weight,
    out,
    xpad,
    form,
    by_wave,
    by_chunk,
    near_mats,
    x2,
    lhs,
    acc,
    cos_all,
    sin_all,
    partial,
    sibling,
    send1,
    recv1,
    recv2,
    waves_in,
    local_sem,
    halo_send,
    halo_recv,
    s0,
    r0,
    s1,
    r1,
    s2,
    r2,
    s3,
    r3,
):
    n_row, n_col, rows, cols, sources, waves, unknowns = dims
    pillars = rows * cols
    share = sources
    pairs = n_row // 2
    me_row, me_col = lax.axis_index("row"), lax.axis_index("col")
    half_cols = n_col // 2
    inner = [(0, 0), (half_cols, 1)]
    outer = list(range(1, half_cols))
    me_q = lax.div(me_col, half_cols)
    me_slot = 2 * me_row + me_q
    peers = 2 * n_row - 1
    my_pair, me_core = lax.div(me_row, 2), lax.rem(me_row, 2)
    chip_slot = 2 * my_pair + me_q
    chip_peers = 2 * pairs - 1
    row_mod, col_mod = Q * rows * n_row, Q * cols * n_col

    def at(row_step, col_step):
        return (lax.rem(me_row + row_step + n_row, n_row), lax.rem(me_col + col_step + n_col, n_col))

    loads = [
        pltpu.make_async_copy(field, xpad.at[1 : rows + 1, 1 : cols + 1], local_sem.at[0]),
        pltpu.make_async_copy(wave_form, form, local_sem.at[1]),
    ]
    for variant in range(2):
        for part in range(2):
            which = 2 * variant + part
            loads.append(
                pltpu.make_async_copy(
                    near_kernel.at[:, variant, part],
                    near_mats.at[:, :, which * unknowns : (which + 1) * unknowns],
                    local_sem.at[2 + which],
                )
            )
    for load in loads:
        load.start()

    barrier = pltpu.get_barrier_semaphore()

    def greet(row, col):
        pl.semaphore_signal(barrier, inc=1, device_id=(row, col), device_id_type=MESH)

    def greet_row(step, _):
        row = lax.rem(me_row + step, n_row)
        for flip, _q in inner:
            greet(row, jnp.bitwise_xor(me_col, flip))
        return 0

    steps = [(0, -1), (0, 1), (-1, 0), (1, 0)]
    sideways = steps[:2]
    for flip in outer:
        greet(me_row, jnp.bitwise_xor(me_col, flip))
    for row_step, col_step in sideways:
        greet(*at(row_step, col_step))
    lax.fori_loop(1, n_row, greet_row, 0)
    for flip, _q in inner[1:]:
        greet(me_row, jnp.bitwise_xor(me_col, flip))

    down = lax.broadcasted_iota(jnp.int32, (pillars, LANES), 0)
    fine_row = jnp.zeros((pillars, LANES), jnp.int32)
    fine_col = jnp.zeros((pillars, LANES), jnp.int32)
    for p in range(pillars):
        r, c = divmod(p, cols)
        fine_row = jnp.where(down == p, Q * (me_row * rows + r) + shift[r, 0, c], fine_row)
        fine_col = jnp.where(down == p, Q * (me_col * cols + c) + shift[r, 1, c], fine_col)
    drift = (BLOCH_ROW / row_mod) * fine_row.astype(jnp.float32) + (
        BLOCH_COL / col_mod
    ) * fine_col.astype(jnp.float32)

    def phases(j, _):
        here = pl.ds(pl.multiple_of(j * LANES, LANES), LANES)
        m = wave_index[0:1, here]
        n = wave_index[1:2, here]
        turn_row = ((m * fine_row) & (row_mod - 1)).astype(jnp.float32) * (1.0 / row_mod)
        turn_col = ((n * fine_col) & (col_mod - 1)).astype(jnp.float32) * (1.0 / col_mod)
        c, s = turn_to_cos_sin(turn_row + turn_col + drift)
        cos_all[:, here] = c
        sin_all[:, here] = s
        return 0

    lax.fori_loop(0, waves // LANES, phases, 0)

    to = lax.broadcasted_iota(jnp.int32, (2 * LANES, 2 * LANES), 0)
    source = lax.broadcasted_iota(jnp.int32, (2 * LANES, 2 * LANES), 1)
    wanted = jnp.where(to < LANES, 2 * to, 2 * (to - LANES) + 1)
    apart = jnp.where(source == wanted, 1.0, 0.0).astype(jnp.bfloat16)
    loads[1].wait()

    def split(chunk, _):
        for half in range(2):
            first = pl.multiple_of((2 * chunk + half) * LANES, LANES)
            block = form[pl.ds(first, LANES)].reshape(2 * LANES, unknowns)
            rows_apart = jnp.dot(apart, block, preferred_element_type=jnp.float32)
            rows_apart = rows_apart.astype(jnp.bfloat16)
            by_wave[pl.ds(first, LANES), 0:unknowns] = rows_apart[:LANES]
            by_wave[pl.ds(first, LANES), unknowns : 2 * unknowns] = rows_apart[LANES:]
            by_chunk[chunk, half * LANES : (half + 1) * LANES] = rows_apart[:LANES]
            by_chunk[chunk, (2 + half) * LANES : (3 + half) * LANES] = rows_apart[LANES:]
        return 0

    lax.fori_loop(0, pairs, split, 0)

    loads[0].wait()
    for p in range(pillars):
        r, c = divmod(p, cols)
        x = xpad[1 + r, 1 + c]
        real, imag = x[:, :unknowns], x[:, unknowns:]
        base = 2 * sources * p
        x2[base : base + sources, :unknowns] = real
        x2[base : base + sources, unknowns:] = -imag
        x2[base + sources : base + 2 * sources, :unknowns] = imag
        x2[base + sources : base + 2 * sources, unknowns:] = real

    halos = []
    spans = {-1: (slice(0, 1), rows + 1), 1: (slice(rows - 1, rows), 0)}
    col_spans = {-1: (slice(0, 1), cols + 1), 1: (slice(cols - 1, cols), 0)}
    for row_step, col_step in steps:
        if row_step:
            from_row, into = spans[row_step]
            to_row = slice(into, into + 1)
        else:
            from_row, to_row = slice(0, rows), slice(1, rows + 1)
        if col_step:
            from_col, into = col_spans[col_step]
            to_col = slice(into, into + 1)
        else:
            from_col, to_col = slice(0, cols), slice(1, cols + 1)
        k = len(halos)
        halos.append(
            pltpu.make_async_remote_copy(
                src_ref=field.at[from_row, from_col],
                dst_ref=xpad.at[to_row, to_col],
                send_sem=halo_send.at[k],
                recv_sem=halo_recv.at[k],
                device_id=at(row_step, col_step),
                device_id_type=MESH,
            )
        )

    corners = []
    for row_step in (-1, 1):
        from_row, into = spans[row_step]
        for edge in (0, cols + 1):
            k = len(halos) + len(corners)
            corners.append(
                pltpu.make_async_remote_copy(
                    src_ref=xpad.at[1 + from_row.start, edge],
                    dst_ref=xpad.at[into, edge],
                    send_sem=halo_send.at[k],
                    recv_sem=halo_recv.at[k],
                    device_id=at(row_step, 0),
                    device_id_type=MESH,
                )
            )

    def sibling_copy(pair):
        return pltpu.make_async_remote_copy(
            src_ref=partial.at[pair, 1 - me_core],
            dst_ref=sibling.at[pair],
            send_sem=s0.at[pair],
            recv_sem=r0.at[pair],
            device_id=(me_row + 1 - 2 * me_core, me_col),
            device_id_type=MESH,
        )

    def first_copy(pair, flip, q):
        return pltpu.make_async_remote_copy(
            src_ref=send1.at[2 * pair + q],
            dst_ref=recv1.at[chip_slot],
            send_sem=s1,
            recv_sem=r1,
            device_id=(2 * pair + me_core, jnp.bitwise_xor(me_col, flip)),
            device_id_type=MESH,
        )

    def all_first():
        return pltpu.make_async_remote_copy(
            src_ref=send1.at[0:chip_peers],
            dst_ref=recv1.at[0:chip_peers],
            send_sem=s1,
            recv_sem=r1,
            device_id=(me_row, jnp.bitwise_xor(me_col, half_cols)),
            device_id_type=MESH,
        )

    def pair_at(step):
        return lax.rem(my_pair + 1 + step, pairs)

    def project(step, _):
        pair = pair_at(step)
        first = pl.multiple_of(pair * 2 * LANES, 2 * LANES)
        projected = lax.dot_general(
            x2[...],
            by_wave[pl.ds(first, 2 * LANES), :],
            NT,
            preferred_element_type=jnp.float32,
        )
        for half in range(2):
            here = pl.ds(pl.multiple_of(first + half * LANES, LANES), LANES)
            lanes = slice(half * LANES, (half + 1) * LANES)
            real = jnp.zeros((sources, LANES), jnp.float32)
            imag = jnp.zeros((sources, LANES), jnp.float32)
            for p in range(pillars):
                base = 2 * sources * p
                pr = projected[base : base + sources, lanes]
                pi = projected[base + sources : base + 2 * sources, lanes]
                c = cos_all[p : p + 1, here]
                s = sin_all[p : p + 1, here]
                real = real + (c * pr - s * pi)
                imag = imag + (c * pi + s * pr)
            partial[pair, half, :sources] = real
            partial[pair, half, sources:] = imag
        return 0

    def give(step, _):
        sibling_copy(pair_at(step)).start()
        return 0

    def add_and_send(step, _):
        pair = pair_at(step)
        sibling_copy(pair).wait_recv()
        for q in range(2):
            span = slice(q * share, (q + 1) * share)
            send1[2 * pair + q] = partial[pair, me_core, span] + sibling[pair, span]
        for flip, step_q in inner:
            if flip:
                first_copy(pair, flip, jnp.bitwise_xor(me_q, step_q)).start()
            else:

                @pl.when(pair != my_pair)
                def _():
                    first_copy(pair, flip, me_q).start()

        return 0

    def project_and_send(step, _):
        project(step, 0)
        give(step, 0)
        add_and_send(step - AHEAD, 0)
        return 0

    ahead = min(AHEAD, pairs)
    lax.fori_loop(0, ahead, project, 0)
    pl.semaphore_wait(barrier, peers + len(outer) + len(sideways))
    lax.fori_loop(0, ahead, give, 0)
    for halo in halos:
        halo.start()
    lax.fori_loop(ahead, pairs, project_and_send, 0)
    lax.fori_loop(pairs - ahead, pairs, add_and_send, 0)
    recv1[chip_slot] = send1[chip_slot]

    def near_offset(offset):
        a = lax.div(offset, 3)
        b = lax.rem(offset, 3)
        for p in range(pillars):
            r, c = divmod(p, cols)
            x = xpad[r + a, c + b]
            real, imag = x[:, :unknowns], x[:, unknowns:]
            base = 2 * sources * p
            for variant in range(2):
                mask = jnp.where(contact[r, c, offset] == variant, 1.0, 0.0)
                mask = jnp.full((sources, unknowns), mask, jnp.float32).astype(jnp.bfloat16)
                chosen_real, chosen_imag = real * mask, imag * mask
                low = 2 * variant * unknowns
                mid, high = low + unknowns, low + 2 * unknowns
                lhs[base : base + sources, low:mid] = chosen_real
                lhs[base : base + sources, mid:high] = -chosen_imag
                lhs[base + sources : base + 2 * sources, low:mid] = chosen_imag
                lhs[base + sources : base + 2 * sources, mid:high] = chosen_real
        acc[...] += lax.dot_general(
            lhs[...], near_mats[offset], NT, preferred_element_type=jnp.float32
        )

    def near_edge(turn, _):
        near_offset(2 * turn + 1)
        return 0

    def near_corner(turn, _):
        near_offset(2 * turn + 2 * lax.div(turn, 2))
        return 0

    for load in loads[2:]:
        load.wait()
    acc[...] = jnp.zeros_like(acc)
    near_offset(jnp.int32(4))

    all_first().wait_recv()

    def add_chip(pair, total):
        for q in range(2):
            total = total + recv1[2 * pair + q]
        return total

    recv2[0] = lax.fori_loop(0, pairs, add_chip, jnp.zeros((share, LANES), jnp.float32))

    seconds = [
        pltpu.make_async_remote_copy(
            src_ref=recv2.at[0],
            dst_ref=recv2.at[1 + k],
            send_sem=s2.at[k],
            recv_sem=r2.at[k],
            device_id=(me_row, jnp.bitwise_xor(me_col, flip)),
            device_id_type=MESH,
        )
        for k, flip in enumerate(outer)
    ]
    for second in seconds:
        second.start()
    for halo in halos:
        halo.wait_recv()
    for corner in corners:
        corner.start()
    lax.fori_loop(0, 4, near_edge, 0)
    total = recv2[0]
    for k, second in enumerate(seconds):
        second.wait_recv()
        total = total + recv2[1 + k]

    far_scale = math.sqrt(unknowns / (waves * rows * n_row * cols * n_col))
    scale = far_scale * wave_weight[pl.ds(me_row, 1), :]
    waves_in[me_slot] = (scale * total).astype(jnp.bfloat16)
    my_pair_sem = r3.at[my_pair]

    def third_copy(row, flip):
        return pltpu.make_async_remote_copy(
            src_ref=waves_in.at[me_slot],
            dst_ref=waves_in.at[me_slot],
            send_sem=s3,
            recv_sem=my_pair_sem,
            device_id=(row, jnp.bitwise_xor(me_col, flip)),
            device_id_type=MESH,
        )

    def some_third(first, count, sem):
        return pltpu.make_async_remote_copy(
            src_ref=waves_in.at[pl.ds(first, count)],
            dst_ref=waves_in.at[pl.ds(first, count)],
            send_sem=s3,
            recv_sem=sem,
            device_id=(me_row, jnp.bitwise_xor(me_col, half_cols)),
            device_id_type=MESH,
        )

    def hand_row(step, _):
        row = lax.rem(me_row + step, n_row)
        for flip, _q in inner:
            third_copy(row, flip).start()
        return 0

    for flip, _q in inner[1:]:
        third_copy(me_row, flip).start()
    lax.fori_loop(1, n_row, hand_row, 0)
    for corner in corners:
        corner.wait_recv()
    lax.fori_loop(0, 4, near_corner, 0)

    def far_pair(step, _):
        pair = lax.rem(my_pair - step + pairs, pairs)

        @pl.when(step == 0)
        def _():
            some_third(0, 3, my_pair_sem).wait_recv()

        @pl.when(step > 0)
        def _():
            some_third(4 * pair, 4, r3.at[pair]).wait_recv()

        for half in range(2):
            here = pl.ds(pl.multiple_of((2 * pair + half) * LANES, LANES), LANES)
            slot = 2 * (2 * pair + half)
            wr = waves_in[slot].astype(jnp.float32)
            wi = waves_in[slot + 1].astype(jnp.float32)
            low = slice(half * LANES, (half + 1) * LANES)
            high = slice((2 + half) * LANES, (3 + half) * LANES)
            for p in range(pillars):
                base = 2 * sources * p
                c = cos_all[p : p + 1, here]
                s = sin_all[p : p + 1, here]
                sr = (c * wr + s * wi).astype(jnp.bfloat16)
                si = (c * wi - s * wr).astype(jnp.bfloat16)
                x2[base : base + sources, low] = sr
                x2[base : base + sources, high] = si
                x2[base + sources : base + 2 * sources, low] = si
                x2[base + sources : base + 2 * sources, high] = -sr
        acc[...] += jnp.dot(x2[...], by_chunk[pair], preferred_element_type=jnp.float32)
        return 0

    lax.fori_loop(0, pairs, far_pair, 0)
    for p in range(pillars):
        r, c = divmod(p, cols)
        base = 2 * sources * p
        out[r, c, :, :unknowns] = acc[base : base + sources]
        out[r, c, :, unknowns:] = acc[base + sources : base + 2 * sources]

    for halo in halos + corners:
        halo.wait_send()

    def drain(pair, _):
        sibling_copy(pair).wait_send()
        return 0

    lax.fori_loop(0, pairs, drain, 0)
    all_first().wait_send()
    for second in seconds:
        second.wait_send()
    some_third(0, peers, my_pair_sem).wait_send()


def local(field, near_kernel, contact, pillar_shift, wave_index, wave_form, wave_weight):
    rows, cols, sources, width = field.shape
    waves = wave_form.shape[0]
    unknowns = width // 2
    n_row = lax.axis_size("row")
    n_col = lax.axis_size("col")
    share = sources
    pillars = rows * cols
    stacked = 2 * pillars * sources
    pairs = n_row // 2
    assert waves == n_row * LANES
    dims = (n_row, n_col, rows, cols, sources, waves, unknowns)
    vmem = pl.BlockSpec(memory_space=pltpu.VMEM)
    smem = pl.BlockSpec(memory_space=pltpu.SMEM)
    anywhere = pl.BlockSpec(memory_space=pl.ANY)
    dma = pltpu.SemaphoreType.DMA
    bf16, f32 = jnp.bfloat16, jnp.float32
    return pl.pallas_call(
        functools.partial(kernel, dims),
        out_shape=pltpu.VMEM((rows, cols, sources, width), f32),
        in_specs=[anywhere, anywhere, smem, smem, vmem, anywhere, vmem],
        out_specs=vmem,
        scratch_shapes=[
            pltpu.VMEM((rows + 2, cols + 2, sources, width), bf16),
            pltpu.VMEM((waves, 2, unknowns), bf16),
            pltpu.VMEM((waves, width), bf16),
            pltpu.VMEM((pairs, 4 * LANES, unknowns), bf16),
            pltpu.VMEM((9, unknowns, 4 * unknowns), bf16),
            pltpu.VMEM((stacked, width), bf16),
            pltpu.VMEM((stacked, 2 * width), bf16),
            pltpu.VMEM((stacked, unknowns), f32),
            pltpu.VMEM((pillars, waves), f32),
            pltpu.VMEM((pillars, waves), f32),
            pltpu.VMEM((pairs, 2, 2 * sources, LANES), f32),
            pltpu.VMEM((pairs, 2 * sources, LANES), f32),
            pltpu.VMEM((2 * pairs, share, LANES), f32),
            pltpu.VMEM((2 * pairs, share, LANES), f32),
            pltpu.VMEM((n_col // 2, share, LANES), f32),
            pltpu.VMEM((2 * n_row, share, LANES), bf16),
            dma((6,)),
            dma((8,)),
            dma((8,)),
            dma((pairs,)),
            dma((pairs,)),
            dma,
            dma,
            dma((n_col // 2 - 1,)),
            dma((n_col // 2 - 1,)),
            dma,
            dma((pairs,)),
        ],
        compiler_params=pltpu.CompilerParams(
            collective_id=0, has_side_effects=True, vmem_limit_bytes=56 * 1024 * 1024
        ),
        name="bloch_apply",
    )(
        field,
        near_kernel,
        contact,
        pillar_shift.transpose(0, 2, 1),
        wave_index.T,
        wave_form,
        wave_weight.reshape(waves // LANES, LANES),
    )


def solution(mesh):
    placed = (
        P("row", "col", None, None),
        P(),
        P("row", "col", None),
        P("row", "col", None),
        P(),
        P(),
        P(),
    )
    return jax.shard_map(
        local, mesh=mesh, in_specs=placed, out_specs=P("row", "col", None, None), check_vma=False
    )
```

```python
import functools
import math

import jax
import jax.numpy as jnp
from jax import lax
from jax.experimental import pallas as pl
from jax.experimental.pallas import tpu as pltpu
from jax.sharding import PartitionSpec as P

Q = 16
LANES = 128
BLOCH_ROW = 0.3
BLOCH_COL = 0.17
MESH = pl.DeviceIdType.MESH
NT = (((1,), (1,)), ((), ()))

AHEAD = 2


def turn_to_cos_sin(turn):
    quarter = jnp.round(turn * 4.0)
    angle = (turn - quarter * 0.25) * (2.0 * math.pi)
    square = angle * angle
    sine = angle * (
        1.0
        + square
        * (-1.0 / 6 + square * (1.0 / 120 + square * (-1.0 / 5040 + square * (1.0 / 362880))))
    )
    cosine = 1.0 + square * (
        -0.5
        + square
        * (1.0 / 24 + square * (-1.0 / 720 + square * (1.0 / 40320 + square * (-1.0 / 3628800))))
    )
    which = quarter.astype(jnp.int32) & 3
    odd = (which & 1) == 1
    c = jnp.where(odd, sine, cosine)
    s = jnp.where(odd, cosine, sine)
    c = jnp.where((which == 1) | (which == 2), -c, c)
    s = jnp.where(which >= 2, -s, s)
    return c, s


def kernel(
    dims,
    field,
    near_kernel,
    contact,
    shift,
    wave_index,
    wave_form,
    wave_weight,
    out,
    xpad,
    form,
    by_wave,
    by_chunk,
    near_mats,
    x2,
    lhs,
    acc,
    cos_all,
    sin_all,
    partial,
    sibling,
    send1,
    recv1,
    recv2,
    waves_in,
    local_sem,
    halo_send,
    halo_recv,
    s0,
    r0,
    s1,
    r1,
    s2,
    r2,
    s3,
    r3,
):
    n_row, n_col, rows, cols, sources, waves, unknowns = dims
    pillars = rows * cols
    share = sources
    pairs = n_row // 2
    me_row, me_col = lax.axis_index("row"), lax.axis_index("col")
    half_cols = n_col // 2
    inner = [(0, 0), (half_cols, 1)]
    outer = sorted(range(1, half_cols), key=lambda flip: -min(flip, half_cols - flip))
    me_q = lax.div(me_col, half_cols)
    me_slot = 2 * me_row + me_q
    peers = 2 * n_row - 1
    my_pair, me_core = lax.div(me_row, 2), lax.rem(me_row, 2)
    chip_slot = 2 * my_pair + me_q
    chip_peers = 2 * pairs - 1
    row_mod, col_mod = Q * rows * n_row, Q * cols * n_col

    def at(row_step, col_step):
        return (lax.rem(me_row + row_step + n_row, n_row), lax.rem(me_col + col_step + n_col, n_col))

    loads = [
        pltpu.make_async_copy(field, xpad.at[1 : rows + 1, 1 : cols + 1], local_sem.at[0]),
        pltpu.make_async_copy(wave_form, form, local_sem.at[1]),
    ]
    for variant in range(2):
        for part in range(2):
            which = 2 * variant + part
            loads.append(
                pltpu.make_async_copy(
                    near_kernel.at[:, variant, part],
                    near_mats.at[:, :, which * unknowns : (which + 1) * unknowns],
                    local_sem.at[2 + which],
                )
            )
    for load in loads:
        load.start()

    barrier = pltpu.get_barrier_semaphore()

    def greet(row, col):
        pl.semaphore_signal(barrier, inc=1, device_id=(row, col), device_id_type=MESH)

    def greet_row(step, _):
        row = lax.rem(me_row + step, n_row)
        for flip, _q in inner:
            greet(row, jnp.bitwise_xor(me_col, flip))
        return 0

    steps = [(0, -1), (0, 1), (-1, 0), (1, 0)]
    sideways = steps[:2]
    for flip in outer:
        greet(me_row, jnp.bitwise_xor(me_col, flip))
    for row_step, col_step in sideways:
        greet(*at(row_step, col_step))
    lax.fori_loop(1, n_row, greet_row, 0)
    for flip, _q in inner[1:]:
        greet(me_row, jnp.bitwise_xor(me_col, flip))

    down = lax.broadcasted_iota(jnp.int32, (pillars, LANES), 0)
    fine_row = jnp.zeros((pillars, LANES), jnp.int32)
    fine_col = jnp.zeros((pillars, LANES), jnp.int32)
    for p in range(pillars):
        r, c = divmod(p, cols)
        fine_row = jnp.where(down == p, Q * (me_row * rows + r) + shift[r, 0, c], fine_row)
        fine_col = jnp.where(down == p, Q * (me_col * cols + c) + shift[r, 1, c], fine_col)
    drift = (BLOCH_ROW / row_mod) * fine_row.astype(jnp.float32) + (
        BLOCH_COL / col_mod
    ) * fine_col.astype(jnp.float32)

    def phases(j, _):
        here = pl.ds(pl.multiple_of(j * LANES, LANES), LANES)
        m = wave_index[0:1, here]
        n = wave_index[1:2, here]
        turn_row = ((m * fine_row) & (row_mod - 1)).astype(jnp.float32) * (1.0 / row_mod)
        turn_col = ((n * fine_col) & (col_mod - 1)).astype(jnp.float32) * (1.0 / col_mod)
        c, s = turn_to_cos_sin(turn_row + turn_col + drift)
        cos_all[:, here] = c
        sin_all[:, here] = s
        return 0

    lax.fori_loop(0, waves // LANES, phases, 0)

    to = lax.broadcasted_iota(jnp.int32, (2 * LANES, 2 * LANES), 0)
    source = lax.broadcasted_iota(jnp.int32, (2 * LANES, 2 * LANES), 1)
    wanted = jnp.where(to < LANES, 2 * to, 2 * (to - LANES) + 1)
    apart = jnp.where(source == wanted, 1.0, 0.0).astype(jnp.bfloat16)
    loads[1].wait()

    def split(chunk, _):
        for half in range(2):
            first = pl.multiple_of((2 * chunk + half) * LANES, LANES)
            block = form[pl.ds(first, LANES)].reshape(2 * LANES, unknowns)
            rows_apart = jnp.dot(apart, block, preferred_element_type=jnp.float32)
            rows_apart = rows_apart.astype(jnp.bfloat16)
            by_wave[pl.ds(first, LANES), 0:unknowns] = rows_apart[:LANES]
            by_wave[pl.ds(first, LANES), unknowns : 2 * unknowns] = rows_apart[LANES:]
            by_chunk[chunk, half * LANES : (half + 1) * LANES] = rows_apart[:LANES]
            by_chunk[chunk, (2 + half) * LANES : (3 + half) * LANES] = rows_apart[LANES:]
        return 0

    lax.fori_loop(0, pairs, split, 0)

    loads[0].wait()
    for p in range(pillars):
        r, c = divmod(p, cols)
        x = xpad[1 + r, 1 + c]
        real, imag = x[:, :unknowns], x[:, unknowns:]
        base = 2 * sources * p
        x2[base : base + sources, :unknowns] = real
        x2[base : base + sources, unknowns:] = -imag
        x2[base + sources : base + 2 * sources, :unknowns] = imag
        x2[base + sources : base + 2 * sources, unknowns:] = real

    halos = []
    spans = {-1: (slice(0, 1), rows + 1), 1: (slice(rows - 1, rows), 0)}
    col_spans = {-1: (slice(0, 1), cols + 1), 1: (slice(cols - 1, cols), 0)}
    for row_step, col_step in steps:
        if row_step:
            from_row, into = spans[row_step]
            to_row = slice(into, into + 1)
        else:
            from_row, to_row = slice(0, rows), slice(1, rows + 1)
        if col_step:
            from_col, into = col_spans[col_step]
            to_col = slice(into, into + 1)
        else:
            from_col, to_col = slice(0, cols), slice(1, cols + 1)
        k = len(halos)
        halos.append(
            pltpu.make_async_remote_copy(
                src_ref=field.at[from_row, from_col],
                dst_ref=xpad.at[to_row, to_col],
                send_sem=halo_send.at[k],
                recv_sem=halo_recv.at[k],
                device_id=at(row_step, col_step),
                device_id_type=MESH,
            )
        )

    corners = []
    for row_step in (-1, 1):
        from_row, into = spans[row_step]
        for edge in (0, cols + 1):
            k = len(halos) + len(corners)
            corners.append(
                pltpu.make_async_remote_copy(
                    src_ref=xpad.at[1 + from_row.start, edge],
                    dst_ref=xpad.at[into, edge],
                    send_sem=halo_send.at[k],
                    recv_sem=halo_recv.at[k],
                    device_id=at(row_step, 0),
                    device_id_type=MESH,
                )
            )

    def sibling_copy(pair):
        return pltpu.make_async_remote_copy(
            src_ref=partial.at[pair, 1 - me_core],
            dst_ref=sibling.at[pair],
            send_sem=s0.at[pair],
            recv_sem=r0.at[pair],
            device_id=(me_row + 1 - 2 * me_core, me_col),
            device_id_type=MESH,
        )

    def first_copy(pair, flip, q):
        return pltpu.make_async_remote_copy(
            src_ref=send1.at[2 * pair + q],
            dst_ref=recv1.at[chip_slot],
            send_sem=s1,
            recv_sem=r1,
            device_id=(2 * pair + me_core, jnp.bitwise_xor(me_col, flip)),
            device_id_type=MESH,
        )

    def all_first():
        return pltpu.make_async_remote_copy(
            src_ref=send1.at[0:chip_peers],
            dst_ref=recv1.at[0:chip_peers],
            send_sem=s1,
            recv_sem=r1,
            device_id=(me_row, jnp.bitwise_xor(me_col, half_cols)),
            device_id_type=MESH,
        )

    def pair_at(step):
        return lax.rem(my_pair + 1 + step, pairs)

    def project(step, _):
        pair = pair_at(step)
        first = pl.multiple_of(pair * 2 * LANES, 2 * LANES)
        projected = lax.dot_general(
            x2[...],
            by_wave[pl.ds(first, 2 * LANES), :],
            NT,
            preferred_element_type=jnp.float32,
        )
        for half in range(2):
            here = pl.ds(pl.multiple_of(first + half * LANES, LANES), LANES)
            lanes = slice(half * LANES, (half + 1) * LANES)
            real = jnp.zeros((sources, LANES), jnp.float32)
            imag = jnp.zeros((sources, LANES), jnp.float32)
            for p in range(pillars):
                base = 2 * sources * p
                pr = projected[base : base + sources, lanes]
                pi = projected[base + sources : base + 2 * sources, lanes]
                c = cos_all[p : p + 1, here]
                s = sin_all[p : p + 1, here]
                real = real + (c * pr - s * pi)
                imag = imag + (c * pi + s * pr)
            partial[pair, half, :sources] = real
            partial[pair, half, sources:] = imag
        return 0

    def give(step, _):
        sibling_copy(pair_at(step)).start()
        return 0

    def add_and_send(step, _):
        pair = pair_at(step)
        sibling_copy(pair).wait_recv()
        for q in range(2):
            span = slice(q * share, (q + 1) * share)
            send1[2 * pair + q] = partial[pair, me_core, span] + sibling[pair, span]
        for flip, step_q in inner:
            if flip:
                first_copy(pair, flip, jnp.bitwise_xor(me_q, step_q)).start()
            else:

                @pl.when(pair != my_pair)
                def _():
                    first_copy(pair, flip, me_q).start()

        return 0

    def project_and_send(step, _):
        project(step, 0)
        give(step, 0)
        add_and_send(step - AHEAD, 0)
        return 0

    ahead = min(AHEAD, pairs)
    lax.fori_loop(0, ahead, project, 0)
    pl.semaphore_wait(barrier, peers + len(outer) + len(sideways))
    lax.fori_loop(0, ahead, give, 0)
    for halo in halos:
        halo.start()
    lax.fori_loop(ahead, pairs, project_and_send, 0)
    lax.fori_loop(pairs - ahead, pairs, add_and_send, 0)
    recv1[chip_slot] = send1[chip_slot]

    def near_offset(offset):
        a = lax.div(offset, 3)
        b = lax.rem(offset, 3)
        for p in range(pillars):
            r, c = divmod(p, cols)
            x = xpad[r + a, c + b]
            real, imag = x[:, :unknowns], x[:, unknowns:]
            base = 2 * sources * p
            for variant in range(2):
                mask = jnp.where(contact[r, c, offset] == variant, 1.0, 0.0)
                mask = jnp.full((sources, unknowns), mask, jnp.float32).astype(jnp.bfloat16)
                chosen_real, chosen_imag = real * mask, imag * mask
                low = 2 * variant * unknowns
                mid, high = low + unknowns, low + 2 * unknowns
                lhs[base : base + sources, low:mid] = chosen_real
                lhs[base : base + sources, mid:high] = -chosen_imag
                lhs[base + sources : base + 2 * sources, low:mid] = chosen_imag
                lhs[base + sources : base + 2 * sources, mid:high] = chosen_real
        acc[...] += lax.dot_general(
            lhs[...], near_mats[offset], NT, preferred_element_type=jnp.float32
        )

    def near_edge(turn, _):
        near_offset(2 * turn + 1)
        return 0

    def near_corner(turn, _):
        near_offset(2 * turn + 2 * lax.div(turn, 2))
        return 0

    for load in loads[2:]:
        load.wait()
    acc[...] = jnp.zeros_like(acc)
    near_offset(jnp.int32(4))

    all_first().wait_recv()

    def add_chip(pair, total):
        for q in range(2):
            total = total + recv1[2 * pair + q]
        return total

    recv2[0] = lax.fori_loop(0, pairs, add_chip, jnp.zeros((share, LANES), jnp.float32))

    seconds = [
        pltpu.make_async_remote_copy(
            src_ref=recv2.at[0],
            dst_ref=recv2.at[1 + k],
            send_sem=s2.at[k],
            recv_sem=r2.at[k],
            device_id=(me_row, jnp.bitwise_xor(me_col, flip)),
            device_id_type=MESH,
        )
        for k, flip in enumerate(outer)
    ]
    for second in seconds:
        second.start()
    for halo in halos:
        halo.wait_recv()
    for corner in corners:
        corner.start()
    lax.fori_loop(0, 4, near_edge, 0)
    total = recv2[0]
    for k, second in enumerate(seconds):
        second.wait_recv()
        total = total + recv2[1 + k]

    far_scale = math.sqrt(unknowns / (waves * rows * n_row * cols * n_col))
    scale = far_scale * wave_weight[pl.ds(me_row, 1), :]
    waves_in[me_slot] = (scale * total).astype(jnp.bfloat16)
    my_pair_sem = r3.at[my_pair]

    def third_copy(row, flip):
        return pltpu.make_async_remote_copy(
            src_ref=waves_in.at[me_slot],
            dst_ref=waves_in.at[me_slot],
            send_sem=s3,
            recv_sem=my_pair_sem,
            device_id=(row, jnp.bitwise_xor(me_col, flip)),
            device_id_type=MESH,
        )

    def some_third(first, count, sem):
        return pltpu.make_async_remote_copy(
            src_ref=waves_in.at[pl.ds(first, count)],
            dst_ref=waves_in.at[pl.ds(first, count)],
            send_sem=s3,
            recv_sem=sem,
            device_id=(me_row, jnp.bitwise_xor(me_col, half_cols)),
            device_id_type=MESH,
        )

    def hand_row(step, _):
        row = lax.rem(me_row + step, n_row)
        for flip, _q in inner:
            third_copy(row, flip).start()
        return 0

    for flip, _q in inner[1:]:
        third_copy(me_row, flip).start()
    lax.fori_loop(1, n_row, hand_row, 0)
    for corner in corners:
        corner.wait_recv()
    lax.fori_loop(0, 4, near_corner, 0)

    def far_pair(step, _):
        pair = lax.rem(my_pair - step + pairs, pairs)

        @pl.when(step == 0)
        def _():
            some_third(0, 3, my_pair_sem).wait_recv()

        @pl.when(step > 0)
        def _():
            some_third(4 * pair, 4, r3.at[pair]).wait_recv()

        for half in range(2):
            here = pl.ds(pl.multiple_of((2 * pair + half) * LANES, LANES), LANES)
            slot = 2 * (2 * pair + half)
            wr = waves_in[slot].astype(jnp.float32)
            wi = waves_in[slot + 1].astype(jnp.float32)
            low = slice(half * LANES, (half + 1) * LANES)
            high = slice((2 + half) * LANES, (3 + half) * LANES)
            for p in range(pillars):
                base = 2 * sources * p
                c = cos_all[p : p + 1, here]
                s = sin_all[p : p + 1, here]
                sr = (c * wr + s * wi).astype(jnp.bfloat16)
                si = (c * wi - s * wr).astype(jnp.bfloat16)
                x2[base : base + sources, low] = sr
                x2[base : base + sources, high] = si
                x2[base + sources : base + 2 * sources, low] = si
                x2[base + sources : base + 2 * sources, high] = -sr
        acc[...] += jnp.dot(x2[...], by_chunk[pair], preferred_element_type=jnp.float32)
        return 0

    lax.fori_loop(0, pairs, far_pair, 0)
    for p in range(pillars):
        r, c = divmod(p, cols)
        base = 2 * sources * p
        out[r, c, :, :unknowns] = acc[base : base + sources]
        out[r, c, :, unknowns:] = acc[base + sources : base + 2 * sources]

    for halo in halos + corners:
        halo.wait_send()

    def drain(pair, _):
        sibling_copy(pair).wait_send()
        return 0

    lax.fori_loop(0, pairs, drain, 0)
    all_first().wait_send()
    for second in seconds:
        second.wait_send()
    some_third(0, peers, my_pair_sem).wait_send()


def local(field, near_kernel, contact, pillar_shift, wave_index, wave_form, wave_weight):
    rows, cols, sources, width = field.shape
    waves = wave_form.shape[0]
    unknowns = width // 2
    n_row = lax.axis_size("row")
    n_col = lax.axis_size("col")
    share = sources
    pillars = rows * cols
    stacked = 2 * pillars * sources
    pairs = n_row // 2
    assert waves == n_row * LANES
    dims = (n_row, n_col, rows, cols, sources, waves, unknowns)
    vmem = pl.BlockSpec(memory_space=pltpu.VMEM)
    smem = pl.BlockSpec(memory_space=pltpu.SMEM)
    anywhere = pl.BlockSpec(memory_space=pl.ANY)
    dma = pltpu.SemaphoreType.DMA
    bf16, f32 = jnp.bfloat16, jnp.float32
    return pl.pallas_call(
        functools.partial(kernel, dims),
        out_shape=pltpu.VMEM((rows, cols, sources, width), f32),
        in_specs=[anywhere, anywhere, smem, smem, vmem, anywhere, vmem],
        out_specs=vmem,
        scratch_shapes=[
            pltpu.VMEM((rows + 2, cols + 2, sources, width), bf16),
            pltpu.VMEM((waves, 2, unknowns), bf16),
            pltpu.VMEM((waves, width), bf16),
            pltpu.VMEM((pairs, 4 * LANES, unknowns), bf16),
            pltpu.VMEM((9, unknowns, 4 * unknowns), bf16),
            pltpu.VMEM((stacked, width), bf16),
            pltpu.VMEM((stacked, 2 * width), bf16),
            pltpu.VMEM((stacked, unknowns), f32),
            pltpu.VMEM((pillars, waves), f32),
            pltpu.VMEM((pillars, waves), f32),
            pltpu.VMEM((pairs, 2, 2 * sources, LANES), f32),
            pltpu.VMEM((pairs, 2 * sources, LANES), f32),
            pltpu.VMEM((2 * pairs, share, LANES), f32),
            pltpu.VMEM((2 * pairs, share, LANES), f32),
            pltpu.VMEM((n_col // 2, share, LANES), f32),
            pltpu.VMEM((2 * n_row, share, LANES), bf16),
            dma((6,)),
            dma((8,)),
            dma((8,)),
            dma((pairs,)),
            dma((pairs,)),
            dma,
            dma,
            dma((n_col // 2 - 1,)),
            dma((n_col // 2 - 1,)),
            dma,
            dma((pairs,)),
        ],
        compiler_params=pltpu.CompilerParams(
            collective_id=0, has_side_effects=True, vmem_limit_bytes=56 * 1024 * 1024
        ),
        name="bloch_apply",
    )(
        field,
        near_kernel,
        contact,
        pillar_shift.transpose(0, 2, 1),
        wave_index.T,
        wave_form,
        wave_weight.reshape(waves // LANES, LANES),
    )


def solution(mesh):
    placed = (
        P("row", "col", None, None),
        P(),
        P("row", "col", None),
        P("row", "col", None),
        P(),
        P(),
        P(),
    )
    return jax.shard_map(
        local, mesh=mesh, in_specs=placed, out_specs=P("row", "col", None, None), check_vma=False
    )
```
